512 devices in a mesh: seq: 128 (over y, z, core), head: 4 (over x).
Axes of the slice: x: 4, y: 8, z: 8, core: 2. Of those that a mesh axis runs over, the one named last changes fastest.
Arguments:
- tokens: bfloat16 [16384, 2048], P('seq', 'head'), as said below
- w_query: bfloat16 [2048, 1024], P(None, 'head'), may hold values from -0.125 to 0.125
- w_key: bfloat16 [2048, 1024], P(None, 'head')
- w_value: bfloat16 [2048, 1024], P(None, 'head'), may hold values from -0.125 to 0.125
- gate_codes: int32 [16384, 8], P('seq', 'head'), may hold values from 28 to 1572854, as said below
- beta_codes: int32 [16384, 8], P('seq', 'head'), may hold values from 32 to 256
- norm_gain: float32 [128], replicated, may hold values from 0.25 to 1.75
- w_out: bfloat16 [1024, 2048], P('head'), may hold values from -0.1875 to 0.1875
Outputs:
- mixed: bfloat16 [16384, 2048], P('seq', 'head')
The draws below stay inside these ranges and needn't reach their ends.
Inputs may be any that keep to these rules, and one draw needn't show every extreme that they name: `gate_codes`: codes are positive; the sweep's gates are those of one recording, identical law in every draw. `tokens`: activations of order one to ten.
All inputs are finite; a program needn't handle non-finite values.
Results may differ from the reference program's by a relative error of at most 0.0049.
Values may be sent and summed in bfloat16 or wider, within the bound.
A program may use at most 128 MiB of HBM per device.

```python
import math
import jax
import jax.numpy as jnp
from jax import lax

D = 2048
H = 8
HEAD_DIM = 128
SPAN = 64
TOK_DEV = 128
TOKENS = 16384


def draw_tokens(key, part):
    first, second = jax.random.split(key, 2)
    scales = jnp.exp(jax.random.uniform(second, (TOKENS, 1), jnp.float32, 0.0, math.log(10.0))) / 3.0
    starting_quantity = jax.random.normal(first, (TOKENS, D), jnp.float32)
    return (starting_quantity * scales).astype(jnp.bfloat16)


def draw_w_key(key, part):
    first, second = jax.random.split(key, 2)
    exponents = jax.random.uniform(second, (1, H * HEAD_DIM), jnp.float32, 0.0, 0.3)
    column_scales = jnp.exp(-exponents * math.log(10.0))
    starting_quantity = jax.random.normal(first, (D, H * HEAD_DIM), jnp.float32)
    return (starting_quantity * column_scales / math.sqrt(D)).astype(jnp.bfloat16)


def draw_gate_codes(key, part):
    keys = jax.random.split(key, 6)
    order = jax.random.permutation(keys[0], H)
    fast = order < max(1, H // 4)
    starting_quantity = jnp.where(fast, 2 ** 21 // 200, max(1, 2 ** 22 // (9 * TOKENS))).astype(jnp.int32)
    segment_scaling_factor = jax.random.randint(keys[1], (TOKENS // SPAN, 1, H), 1, 4, dtype=jnp.int32)
    segment_scaling_factor = jnp.broadcast_to(segment_scaling_factor, (TOKENS // SPAN, SPAN, H)).reshape(TOKENS, H)
    processor_scaling_factor = jax.random.randint(keys[2], (TOKENS // TOK_DEV, 1, H), 1, 3, dtype=jnp.int32)
    processor_scaling_factor = jnp.broadcast_to(processor_scaling_factor, (TOKENS // TOK_DEV, TOK_DEV, H)).reshape(TOKENS, H)
    frame_scaling_factor = jax.random.randint(keys[3], (TOKENS, H), 1, 3, dtype=jnp.int32)
    location_indices = jax.random.randint(keys[4], (3, 1, H), 0, TOKENS, dtype=jnp.int32)
    portion_counts = jax.random.randint(keys[5], (3, 1, H), 461373, 1447035, dtype=jnp.int32)
    assigned_locations = jnp.arange(TOKENS, dtype=jnp.int32)[None, :, None]
    segment_lengths = jnp.max(jnp.where(assigned_locations == location_indices, portion_counts, 0), axis=0)
    return starting_quantity[None, :] * segment_scaling_factor * processor_scaling_factor * frame_scaling_factor + segment_lengths


def touch_ends(drawn, own_key, least, largest):
    spot = [jax.random.randint(jax.random.fold_in(own_key, axis), (), 0, length) for axis, length in enumerate(drawn.shape)]
    main_axis = drawn.shape.index(max(drawn.shape))
    next_to = spot[:main_axis] + [(spot[main_axis] + 1) % drawn.shape[main_axis]] + spot[main_axis + 1:]
    return drawn.at[tuple(spot)].set(least).at[tuple(next_to)].set(largest)


def steps_of(stream_key, dims, pieces, least, high):
    def one(dim, parts):
        draws = jax.random.uniform(jax.random.fold_in(jax.random.fold_in(stream_key, 6), dim), (parts,), jnp.float32, least / len(pieces), high / len(pieces))
        return jnp.repeat(jnp.exp(draws), dims[dim] // parts).reshape((-1,) + (1,) * (len(dims) - dim - 1))

    level = one(*pieces[0])
    for cut in pieces[1:]:
        level = level * one(*cut)
    return level


def normal_values(own_key, shape, width, most, cuts=(), held_as=jnp.bfloat16):
    result = jax.random.normal(own_key, shape, jnp.float32) * width
    if len(cuts) > 0:
        result = steps_of(own_key, shape, cuts, -0.22, 0.18) * result
    return jnp.clip(result, min=-most, max=most).astype(held_as)


def setup_inputs(seed: int = 0) -> dict:
    arg_keys = jax.random.split(jax.random.key(seed), 9)
    return {
        "tokens": draw_tokens(jax.random.fold_in(arg_keys[8], 71), 0),
        "w_query": normal_values(arg_keys[1], (D, H * HEAD_DIM), D ** -0.5, 0.125, ((1, 4),)),
        "w_key": draw_w_key(jax.random.fold_in(arg_keys[8], 71), 0),
        "w_value": normal_values(arg_keys[3], (D, H * HEAD_DIM), D ** -0.5, 0.125, ((1, 4),)),
        "gate_codes": draw_gate_codes(jax.random.fold_in(arg_keys[8], 71), 0),
        "beta_codes": touch_ends(jax.random.randint(arg_keys[5], (TOKENS, H), 32, 257), jax.random.fold_in(arg_keys[5], 1), 32, 256).astype(jnp.int32),
        "norm_gain": jnp.clip(1.0 + 0.15 * jax.random.normal(arg_keys[6], (HEAD_DIM,), jnp.float32), 0.25, 1.75),
        "w_out": normal_values(arg_keys[7], (H * HEAD_DIM, D), (H * HEAD_DIM) ** -0.5, 0.1875, ((0, 4),)),
    }


def reference(tokens, w_query, w_key, w_value, gate_codes, beta_codes, norm_gain, w_out):
    highest = lax.Precision.HIGHEST
    query = jnp.dot(tokens.astype(jnp.float32), w_query.astype(jnp.float32), preferred_element_type=jnp.float32)
    key_rows = jnp.dot(tokens.astype(jnp.float32), w_key.astype(jnp.float32), preferred_element_type=jnp.float32)
    value = jnp.dot(tokens.astype(jnp.float32), w_value.astype(jnp.float32), preferred_element_type=jnp.float32)
    n_spans = TOKENS // SPAN

    def split_heads(array):
        return array.reshape(n_spans, SPAN, H, HEAD_DIM).transpose(0, 2, 1, 3)
    queries = split_heads(query)
    unit_keys = split_heads(key_rows)
    unit_keys = unit_keys * lax.rsqrt(lax.optimization_barrier(jnp.sum(unit_keys * unit_keys, -1, keepdims=True)) + 1e-06)
    values = split_heads(value)
    decay_log = (-gate_codes.astype(jnp.float32) / 2097152.0).reshape(n_spans, SPAN, H).transpose(0, 2, 1)
    log_decay = jnp.cumsum(decay_log, axis=-1)
    betas = (beta_codes.astype(jnp.float32) / 256.0).reshape(n_spans, SPAN, H).transpose(0, 2, 1)
    positions = jnp.arange(SPAN)
    lower_incl = positions[:, None] >= positions[None, :]
    lower_strict = positions[:, None] > positions[None, :]
    identity_mat = jnp.eye(SPAN, dtype=jnp.float32)

    def span_step(state, inputs):
        span_query, span_key, span_value, span_log, span_beta = inputs
        gaps = span_log[:, :, None] - span_log[:, None, :]
        inclusive = jnp.where(lower_incl, jnp.exp(jnp.where(lower_incl, gaps, 0.0)), 0.0)
        strict = jnp.where(lower_strict, inclusive, 0.0)
        key_dots = jnp.einsum('htd,hid->hti', span_key, span_key, precision=highest)
        system = identity_mat + span_beta[:, :, None] * key_dots * strict
        right = jnp.concatenate([span_beta[:, :, None] * span_key * jnp.exp(span_log)[:, :, None], span_beta[:, :, None] * span_value], axis=-1)
        solved = jax.scipy.linalg.solve_triangular(system, right, lower=True, unit_diagonal=True)
        wy_keys = solved[..., :HEAD_DIM]
        wy_values = solved[..., HEAD_DIM:]
        pseudo = wy_values - jnp.einsum('htk,hvk->htv', wy_keys, state, precision=highest)
        query_dots = jnp.einsum('htd,hid->hti', span_query, span_key, precision=highest) * inclusive
        span_out = jnp.einsum('htk,hvk->htv', span_query * jnp.exp(span_log)[:, :, None], state, precision=highest)
        span_out = span_out + jnp.einsum('hti,hiv->htv', query_dots, pseudo, precision=highest)
        last_log = span_log[:, -1]
        key_tail = span_key * jnp.exp(last_log[:, None] - span_log)[:, :, None]
        new_state = jnp.exp(last_log)[:, None, None] * state + jnp.einsum('htv,htk->hvk', pseudo, key_tail, precision=highest)
        return (new_state, span_out)
    start_state = jnp.zeros((H, HEAD_DIM, HEAD_DIM), jnp.float32)
    _, outputs = lax.scan(span_step, start_state, (queries, unit_keys, values, log_decay, betas))
    normed = outputs * lax.rsqrt(lax.optimization_barrier(jnp.mean(outputs * outputs, -1, keepdims=True)) + 1e-06) * norm_gain
    normed = normed.astype(jnp.bfloat16).transpose(0, 2, 1, 3).reshape(TOKENS, H * HEAD_DIM)
    return jnp.dot(normed.astype(jnp.float32), w_out.astype(jnp.float32), preferred_element_type=jnp.float32).astype(jnp.bfloat16)
```

```python
import functools
import jax
import jax.numpy as jnp
from jax import lax
from jax.experimental import pallas as pl
from jax.experimental.pallas import tpu as pltpu
from jax.sharding import PartitionSpec as P

MESH = pl.DeviceIdType.MESH
WIRE = jnp.bfloat16
F32 = jnp.float32
BF16 = jnp.bfloat16


def mm(a, b, dims=((1,), (0,))):
    return lax.dot_general(a, b, (dims, ((), ())), preferred_element_type=F32)


def halves(a):
    high = a.astype(BF16)
    return high, (a - high.astype(F32)).astype(BF16)


def dot3(a, b, dims=((1,), (0,))):
    a_high, a_low = halves(a)
    b_high, b_low = halves(b)
    return mm(a_high, b_high, dims) + (mm(a_high, b_low, dims) + mm(a_low, b_high, dims))


def dot2(a, b):
    a_high, a_low = halves(a)
    return mm(a_high, b) + mm(a_low, b)


def by_map(a, b):
    return dot2(a, b) if b.dtype == BF16 else dot3(a, b)


def below(top, rows):
    return jnp.concatenate([jnp.zeros((top, rows.shape[1]), F32), rows.astype(F32)], axis=0)


def unit_inverse(low, rows, cols):
    size = low.shape[0]
    eye = (rows == cols).astype(F32)
    base = jnp.where(rows // 8 == cols // 8, low, 0.0)
    square = dot3(base, base)
    fourth = dot3(square, square)
    result = dot3(dot3(eye - base, eye + square), eye + fourth)
    width = 8
    while width < size:
        mask = (rows // (2 * width) == cols // (2 * width)) & (rows // width > cols // width)
        corner = jnp.where(mask, low, 0.0)
        result = result - dot3(dot3(result, corner), result)
        width *= 2
    return result


def kernel(
    nx, ny, nz,
    tok_ref, wq_hbm, wk_hbm, wv_hbm, gate_ref, beta_ref, gain_ref, wo_hbm,
    out_ref,
    tok_all, wq, wk, wv, wo_all, ex_send, ex_recv, gz, gy, st_send, st_recv, norm_all, eff, intra,
    load_sem, x_send, x_recv, wo_send, wo_recv, n_send, n_recv, core_send, core_recv,
    z_send, z_recv, y_send, y_recv,
):
    index = lax.axis_index("seq")
    x = lax.axis_index("head")
    core = index % 2
    z = (index // 2) % nz
    y = index // (2 * nz)
    size = gain_ref.shape[1]
    n_tok, width = tok_ref.shape
    out_cols = out_ref.shape[1]

    def at(y_to, z_to, core_to, x_to):
        return ((y_to * nz + z_to) * 2 + core_to, x_to)

    x_right, x_left = at(y, z, core, (x + 1) % nx), at(y, z, core, (x + nx - 1) % nx)
    z_right, z_left = at(y, (z + 1) % nz, core, x), at(y, (z + nz - 1) % nz, core, x)
    y_right, y_left = at((y + 1) % ny, z, core, x), at((y + ny - 1) % ny, z, core, x)
    partner = at(y, z, 1 - core, x)

    loads = [
        pltpu.make_async_copy(source, target, load_sem.at[i])
        for i, (source, target) in enumerate(((wq_hbm, wq), (wk_hbm, wk), (wv_hbm, wv)))
    ]
    for load in loads:
        load.start()
    own_cols = pl.ds(pl.multiple_of(x * out_cols, 128), out_cols)
    own_out = pltpu.make_async_copy(wo_hbm.at[:, own_cols], wo_all.at[x], load_sem.at[3])
    own_out.start()

    friends = [at(y, z, core, (x + d) % nx) for d in range(1, nx)]
    friends += [partner]
    friends += [z_right] + ([z_left] if nz > 2 else [])
    friends += [y_right] + ([y_left] if ny > 2 else [])
    barrier = pltpu.get_barrier_semaphore()
    for friend in friends:
        pl.semaphore_signal(barrier, inc=1, device_id=friend, device_id_type=MESH)
    pl.semaphore_wait(barrier, len(friends))

    def send(source, target, s_sem, r_sem, to):
        return pltpu.make_async_remote_copy(
            src_ref=source, dst_ref=target, send_sem=s_sem, recv_sem=r_sem,
            device_id=to, device_id_type=MESH,
        )

    def x_gather(own, slots, s_sems, r_sems, use):
        half = own.shape[0] // 2
        before, after, across = (x + nx - 1) % nx, (x + 1) % nx, (x + 2) % nx
        first = send(own, slots.at[x], s_sems.at[0], r_sems.at[0], x_right)
        second = send(own, slots.at[x], s_sems.at[1], r_sems.at[1], x_left)
        first.start()
        second.start()
        use(x, own[...])
        first.wait_recv()
        top = slots.at[before, pl.ds(0, half)]
        third = send(top, top, s_sems.at[2], r_sems.at[2], x_right)
        third.start()
        second.wait_recv()
        low = slots.at[after, pl.ds(half, half)]
        fourth = send(low, low, s_sems.at[3], r_sems.at[3], x_left)
        fourth.start()
        use(before, slots[before])
        use(after, slots[after])
        third.wait_recv()
        fourth.wait_recv()
        use(across, slots[across])
        for copy in (first, second, third, fourth):
            copy.wait_send()

    sums = [jnp.zeros((n_tok, wq.shape[1]), F32) for _ in range(3)]
    loaded = []

    def project(place, block):
        if not loaded:
            for load in loads:
                load.wait()
            loaded.append(True)
        part = pl.ds(pl.multiple_of(place * width, 128), width)
        for i, weight in enumerate((wq, wk, wv)):
            sums[i] = sums[i] + mm(block, weight[part, :])

    x_gather(tok_ref, tok_all, x_send, x_recv, project)

    own_out.wait()
    out_copies = []
    for d in range(1, nx):
        there = (x + d) % nx
        cols = pl.ds(pl.multiple_of(there * out_cols, 128), out_cols)
        out_copies.append(
            send(wo_hbm.at[:, cols], wo_all.at[x], wo_send.at[d - 1], wo_recv.at[d - 1],
                 at(y, z, core, there))
        )
    for copy in out_copies:
        copy.start()

    rows = lax.broadcasted_iota(jnp.int32, (n_tok, n_tok), 0)
    cols = lax.broadcasted_iota(jnp.int32, (n_tok, n_tok), 1)
    lower = rows >= cols
    ones_low = lower.astype(BF16)
    maps = []
    for head in range(2):
        cut = slice(head * size, (head + 1) * size)
        query, key, value = (s[:, cut] for s in sums)
        key = key * lax.rsqrt(jnp.sum(key * key, -1, keepdims=True) + 1e-06)
        code = -gate_ref[:, head : head + 1].astype(F32) / 2097152.0
        beta = beta_ref[:, head : head + 1].astype(F32) / 256.0
        spread = jnp.broadcast_to(code, (n_tok, n_tok))
        c_high, c_low = halves(spread)
        c_last = (spread - c_high.astype(F32) - c_low.astype(F32)).astype(BF16)
        logs = mm(ones_low, c_high) + (mm(ones_low, c_low) + mm(ones_low, c_last))
        gaps = logs - logs.T
        incl = jnp.where(lower, jnp.exp(jnp.where(lower, gaps, 0.0)), 0.0)
        strict = jnp.where(rows > cols, incl, 0.0)
        log = logs[:, 0:1]
        last = logs[n_tok - 1 : n_tok, 0:1]
        low = beta * dot3(key, key, ((1,), (1,))) * strict
        inverse = unit_inverse(low, rows, cols)
        right = jnp.concatenate([beta * key * jnp.exp(log), beta * value], axis=1)
        solved = dot3(inverse, right)
        dots = dot3(query, key, ((1,), (1,))) * incl
        inner = dot3(dots, solved)
        intra[head] = inner[:, size:]
        eff[head] = query * jnp.exp(log) - inner[:, :size]
        tail = key * jnp.exp(last - log)
        signed = jnp.concatenate([-solved[:, :size], solved[:, size:]], axis=1)
        moved = dot3(signed, tail, ((0,), (0,)))
        r2 = lax.broadcasted_iota(jnp.int32, (2 * size, size), 0)
        c2 = lax.broadcasted_iota(jnp.int32, (2 * size, size), 1)
        maps.append(moved + jnp.where(r2 == c2, jnp.exp(last), 0.0))

    first_core = core == 0
    ex_send[...] = jnp.where(first_core, maps[1], maps[0])
    swap = send(ex_send, ex_recv, core_send.at[0], core_recv.at[0], partner)
    swap.start()
    mine = jnp.where(first_core, maps[0], maps[1])
    swap.wait_recv()
    other = ex_recv[...]
    early = jnp.where(first_core, mine, other)
    late = jnp.where(first_core, other, mine)
    gz[z] = (dot3(early, late[:size]) + below(size, late[size:])).astype(WIRE)

    def ring(slots, place, count, s_sems, r_sems, right_id, left_id):
        ahead, behind = count // 2, count - 1 - count // 2
        started = []
        rights, lefts = [], []
        for step in range(max(ahead, behind)):
            if step < ahead:
                slot = (place + count - step) % count
                if step:
                    rights[-1].wait_recv()
                copy = send(slots.at[slot], slots.at[slot], s_sems.at[0, step], r_sems.at[0, step], right_id)
                copy.start()
                rights.append(copy)
            if step < behind:
                slot = (place + step) % count
                if step:
                    lefts[-1].wait_recv()
                copy = send(slots.at[slot], slots.at[slot], s_sems.at[1, step], r_sems.at[1, step], left_id)
                copy.start()
                lefts.append(copy)
        for copies in (rights, lefts):
            if copies:
                copies[-1].wait_recv()
            started += copies
        return started

    z_copies = ring(gz, z, nz, z_send, z_recv, z_right, z_left)
    total = gz[0].astype(F32)
    r2 = lax.broadcasted_iota(jnp.int32, (2 * size, size), 0)
    c2 = lax.broadcasted_iota(jnp.int32, (2 * size, size), 1)
    prefix = (r2 == c2).astype(F32)
    for j in range(1, nz):
        prefix = jnp.where(z == j, total, prefix)
        nxt = gz[j]
        total = by_map(total, nxt[:size]) + below(size, nxt[size:])
    gy[y] = total.astype(WIRE)
    y_copies = ring(gy, y, ny, y_send, y_recv, y_right, y_left)
    state = jnp.zeros((size, size), F32)
    for j in range(ny - 1):
        nxt = gy[j]
        state = jnp.where(y > j, by_map(state, nxt[:size]) + nxt[size:].astype(F32), state)
    chip = dot3(state, prefix[:size]) + prefix[size:]
    second = dot3(chip, early[:size]) + early[size:]
    st_send[...] = jnp.where(first_core, second, chip)
    give = send(st_send, st_recv, core_send.at[1], core_recv.at[1], partner)
    give.start()
    kept = jnp.where(first_core, chip, second)
    give.wait_recv()
    got = st_recv[...]
    states = [jnp.where(first_core, kept, got), jnp.where(first_core, got, kept)]
    gain = gain_ref[...]
    for head in range(2):
        o = intra[head] + dot3(eff[head], states[head], ((1,), (1,)))
        scale = lax.rsqrt(jnp.mean(o * o, -1, keepdims=True) + 1e-06)
        norm_all[x, :, head * size : (head + 1) * size] = (o * scale * gain).astype(BF16)

    result = [jnp.zeros((n_tok, out_cols), F32)]
    arrived = []

    def finish(place, block):
        if len(arrived) == 1:
            for copy in out_copies:
                copy.wait_recv()
        arrived.append(True)
        result[0] = result[0] + mm(block, wo_all[place])

    x_gather(norm_all.at[x], norm_all, n_send, n_recv, finish)
    out_ref[...] = result[0].astype(BF16)
    for copy in out_copies + z_copies + y_copies + [swap, give]:
        copy.wait_send()


def shards(ny, nz, nx, tokens, w_query, w_key, w_value, gate_codes, beta_codes, norm_gain, w_out):
    n_tok, width = tokens.shape
    size = norm_gain.shape[0]
    here = w_query.shape[1]
    vmem = pl.BlockSpec(memory_space=pltpu.VMEM)
    hbm = pl.BlockSpec(memory_space=pl.ANY)
    dma = pltpu.SemaphoreType.DMA
    return pl.pallas_call(
        functools.partial(kernel, nx, ny, nz),
        out_shape=jax.ShapeDtypeStruct((n_tok, w_out.shape[1] // nx), BF16),
        in_specs=[vmem, hbm, hbm, hbm, vmem, vmem, vmem, hbm],
        out_specs=vmem,
        scratch_shapes=[
            pltpu.VMEM((nx, n_tok, width), BF16),
            pltpu.VMEM(w_query.shape, BF16),
            pltpu.VMEM(w_key.shape, BF16),
            pltpu.VMEM(w_value.shape, BF16),
            pltpu.VMEM((nx, here, w_out.shape[1] // nx), BF16),
            pltpu.VMEM((2 * size, size), F32),
            pltpu.VMEM((2 * size, size), F32),
            pltpu.VMEM((nz, 2 * size, size), WIRE),
            pltpu.VMEM((ny, 2 * size, size), WIRE),
            pltpu.VMEM((size, size), F32),
            pltpu.VMEM((size, size), F32),
            pltpu.VMEM((nx, n_tok, here), BF16),
            pltpu.VMEM((2, n_tok, size), F32),
            pltpu.VMEM((2, n_tok, size), F32),
            dma((4,)), dma((4,)), dma((4,)), dma((nx - 1,)), dma((nx - 1,)), dma((4,)), dma((4,)),
            dma((2,)), dma((2,)), dma((2, nz)), dma((2, nz)), dma((2, ny)), dma((2, ny)),
        ],
        compiler_params=pltpu.CompilerParams(
            collective_id=0, has_side_effects=True, vmem_limit_bytes=40 << 20
        ),
    )(tokens, w_query, w_key, w_value, gate_codes, beta_codes, norm_gain.reshape(1, size), w_out)


def solution(mesh):
    chips = mesh.shape["seq"] // 2
    nz = 1
    while nz * nz < chips:
        nz *= 2
    return jax.shard_map(
        functools.partial(shards, chips // nz, nz, mesh.shape["head"]),
        mesh=mesh,
        in_specs=(
            P("seq", "head"), P(None, "head"), P(None, "head"), P(None, "head"),
            P("seq", "head"), P("seq", "head"), P(), P("head", None),
        ),
        out_specs=P("seq", "head"),
        check_vma=False,
    )
```

```python
import functools
import jax
import jax.numpy as jnp
from jax import lax
from jax.experimental import pallas as pl
from jax.experimental.pallas import tpu as pltpu
from jax.sharding import PartitionSpec as P

MESH = pl.DeviceIdType.MESH
WIRE = jnp.bfloat16
F32 = jnp.float32
BF16 = jnp.bfloat16


def mm(a, b, dims=((1,), (0,))):
    return lax.dot_general(a, b, (dims, ((), ())), preferred_element_type=F32)


def halves(a):
    high = a.astype(BF16)
    return high, (a - high.astype(F32)).astype(BF16)


def dot3(a, b, dims=((1,), (0,))):
    a_high, a_low = halves(a)
    b_high, b_low = halves(b)
    return mm(a_high, b_high, dims) + (mm(a_high, b_low, dims) + mm(a_low, b_high, dims))


def dot2(a, b):
    a_high, a_low = halves(a)
    return mm(a_high, b) + mm(a_low, b)


def by_map(a, b):
    return dot2(a, b) if b.dtype == BF16 else dot3(a, b)


def below(top, rows):
    return jnp.concatenate([jnp.zeros((top, rows.shape[1]), F32), rows.astype(F32)], axis=0)


def unit_inverse(low, rows, cols):
    size = low.shape[0]
    eye = (rows == cols).astype(F32)
    base = jnp.where(rows // 8 == cols // 8, low, 0.0)
    square = dot3(base, base)
    fourth = dot3(square, square)
    result = dot3(dot3(eye - base, eye + square), eye + fourth)
    width = 8
    while width < size:
        mask = (rows // (2 * width) == cols // (2 * width)) & (rows // width > cols // width)
        corner = jnp.where(mask, low, 0.0)
        result = result - dot3(dot3(result, corner), result)
        width *= 2
    return result


def kernel(
    nx, ny, nz,
    tok_hbm, wq_hbm, wk_hbm, wv_hbm, gate_hbm, beta_hbm, gain_hbm, wo_hbm,
    out_ref,
    tok_all, wq, wk, wv, wo_all, gate_ref, beta_ref, gain_ref, ex_send, ex_recv, gz, gy, st_send, st_recv,
    norm_all, eff, intra,
    load_sem, x_send, x_recv, wo_send, wo_recv, n_send, n_recv, core_send, core_recv,
    z_send, z_recv, y_send, y_recv,
):
    index = lax.axis_index("seq")
    x = lax.axis_index("head")
    core = index % 2
    z = (index // 2) % nz
    y = index // (2 * nz)
    size = gain_ref.shape[1]
    n_tok, width = tok_hbm.shape
    out_cols = out_ref.shape[1]

    def at(y_to, z_to, core_to, x_to):
        return ((y_to * nz + z_to) * 2 + core_to, x_to)

    x_right, x_left = at(y, z, core, (x + 1) % nx), at(y, z, core, (x + nx - 1) % nx)
    z_right, z_left = at(y, (z + 1) % nz, core, x), at(y, (z + nz - 1) % nz, core, x)
    y_right, y_left = at((y + 1) % ny, z, core, x), at((y + ny - 1) % ny, z, core, x)
    partner = at(y, z, 1 - core, x)

    friends = [at(y, z, core, (x + d) % nx) for d in range(1, nx)]
    friends += [partner]
    friends += [z_right] + ([z_left] if nz > 2 else [])
    friends += [y_right] + ([y_left] if ny > 2 else [])
    barrier = pltpu.get_barrier_semaphore()
    for friend in friends:
        pl.semaphore_signal(barrier, inc=1, device_id=friend, device_id_type=MESH)

    own_cols = pl.ds(pl.multiple_of(x * out_cols, 128), out_cols)
    loads = [
        pltpu.make_async_copy(source, target, load_sem.at[i])
        for i, (source, target) in enumerate(
            (
                (tok_hbm, tok_all.at[x]), (gate_hbm, gate_ref), (beta_hbm, beta_ref), (wk_hbm, wk),
                (wv_hbm, wv), (wq_hbm, wq), (gain_hbm, gain_ref), (wo_hbm.at[:, own_cols], wo_all.at[x]),
            )
        )
    ]
    for load in loads:
        load.start()
    pl.semaphore_wait(barrier, len(friends))

    def send(source, target, s_sem, r_sem, to):
        return pltpu.make_async_remote_copy(
            src_ref=source, dst_ref=target, send_sem=s_sem, recv_sem=r_sem,
            device_id=to, device_id_type=MESH,
        )

    def x_gather(own, slots, s_sems, r_sems, use):
        half = own.shape[0] // 2
        before, after, across = (x + nx - 1) % nx, (x + 1) % nx, (x + 2) % nx
        first, second = [], []
        for k, part in enumerate((0, half)):
            other = half - part
            first.append(
                send(own.at[pl.ds(part, half)], slots.at[x, pl.ds(part, half)], s_sems.at[0, k], r_sems.at[0, k], x_right)
            )
            second.append(
                send(own.at[pl.ds(other, half)], slots.at[x, pl.ds(other, half)], s_sems.at[1, k], r_sems.at[1, k], x_left)
            )
            first[k].start()
            second[k].start()
        use(x, None)
        first[0].wait_recv()
        top = slots.at[before, pl.ds(0, half)]
        third = send(top, top, s_sems.at[2, 0], r_sems.at[2, 0], x_right)
        third.start()
        second[0].wait_recv()
        low = slots.at[after, pl.ds(half, half)]
        fourth = send(low, low, s_sems.at[3, 0], r_sems.at[3, 0], x_left)
        fourth.start()
        first[1].wait_recv()
        use(before, slots[before])
        second[1].wait_recv()
        use(after, slots[after])
        third.wait_recv()
        fourth.wait_recv()
        use(across, slots[across])
        return first + second + [third, fourth]

    rows = lax.broadcasted_iota(jnp.int32, (n_tok, n_tok), 0)
    cols = lax.broadcasted_iota(jnp.int32, (n_tok, n_tok), 1)
    lower = rows >= cols
    r2 = lax.broadcasted_iota(jnp.int32, (2 * size, size), 0)
    c2 = lax.broadcasted_iota(jnp.int32, (2 * size, size), 1)
    unit = (r2 == c2).astype(F32)
    heads = range(2)
    logs, incls, betas, lasts = [], [], [], []

    def gates():
        loads[1].wait()
        loads[2].wait()
        ones_up = (rows <= cols).astype(BF16)
        for head in heads:
            code = -gate_ref[head : head + 1, :].astype(F32) / 2097152.0
            beta = beta_ref[head : head + 1, :].astype(F32) / 256.0
            spread = jnp.broadcast_to(code, (n_tok, n_tok))
            c_high, c_low = halves(spread)
            c_last = (spread - c_high.astype(F32) - c_low.astype(F32)).astype(BF16)
            across = mm(c_high, ones_up) + (mm(c_low, ones_up) + mm(c_last, ones_up))
            log = across.T
            gaps = log - across
            logs.append(log)
            incls.append(jnp.where(lower, jnp.exp(jnp.where(lower, gaps, 0.0)), 0.0))
            betas.append(jnp.broadcast_to(beta, (n_tok, n_tok)).T)
            lasts.append(across[0:1, n_tok - 1 : n_tok])

    sums = [jnp.zeros((n_tok, wq.shape[1]), F32) for _ in range(2)]

    def project(place, block):
        if block is None:
            gates()
            loads[0].wait()
            loads[3].wait()
            loads[4].wait()
            block = tok_all[x]
        part = pl.ds(pl.multiple_of(place * width, 128), width)
        for i, weight in enumerate((wk, wv)):
            sums[i] = sums[i] + mm(block, weight[part, :])

    tok_copies = x_gather(tok_hbm, tok_all, x_send, x_recv, project)

    out_copies = []
    for d in range(1, nx):
        there = (x + d) % nx
        there_cols = pl.ds(pl.multiple_of(there * out_cols, 128), out_cols)
        out_copies.append(
            send(wo_hbm.at[:, there_cols], wo_all.at[x], wo_send.at[d - 1], wo_recv.at[d - 1],
                 at(y, z, core, there))
        )
    for copy in out_copies:
        copy.start()

    maps, keys, solves = [], [], []
    for head in heads:
        cut = slice(head * size, (head + 1) * size)
        key, value = (s[:, cut] for s in sums)
        key = key * lax.rsqrt(jnp.sum(key * key, -1, keepdims=True) + 1e-06)
        beta, log, last = betas[head], logs[head], lasts[head]
        low = jnp.where(rows > cols, beta * dot3(key, key, ((1,), (1,))) * incls[head], 0.0)
        inverse = unit_inverse(low, rows, cols)
        right = jnp.concatenate([beta * key * jnp.exp(log), beta * value], axis=1)
        solved = dot3(inverse, right)
        tail = key * jnp.exp(last - log)
        signed = jnp.concatenate([-solved[:, :size], solved[:, size:]], axis=1)
        moved = dot3(signed, tail, ((0,), (0,)))
        maps.append(moved + jnp.where(r2 == c2, jnp.exp(last), 0.0))
        keys.append(key)
        solves.append(solved)

    first_core = core == 0
    ex_send[...] = jnp.where(first_core, maps[1], maps[0])
    swap = send(ex_send, ex_recv, core_send.at[0], core_recv.at[0], partner)
    swap.start()
    mine = jnp.where(first_core, maps[0], maps[1])
    swap.wait_recv()
    other = ex_recv[...]
    early = jnp.where(first_core, mine, other)
    late = jnp.where(first_core, other, mine)
    gz[z] = (dot3(early, late[:size]) + below(size, late[size:])).astype(WIRE)

    def ring(slots, place, count, s_sems, r_sems, to, fill):
        chunks = r_sems.shape[2]
        rows_each = slots.shape[1] // chunks
        far = count // 2
        sent = []
        waiting = {}
        for step in range(far):
            for chunk in range(chunks):
                for way in range(2):
                    if step == far - 1 and (chunk < chunks // 2) != (way == 0):
                        continue
                    if step:
                        waiting.pop((way, step - 1, chunk)).wait_recv()
                    slot = (place + count - step) % count if way == 0 else (place + step) % count
                    piece = slots.at[slot, pl.ds(chunk * rows_each, rows_each)]
                    copy = send(piece, piece, s_sems.at[way, step, chunk], r_sems.at[way, step, chunk], to[way])
                    copy.start()
                    sent.append(copy)
                    waiting[way, step, chunk] = copy
            if step < len(fill):
                fill[step]()
        for copy in waiting.values():
            copy.wait_recv()
        return sent

    queries = []

    def ask():
        loads[5].wait()
        total = jnp.zeros((n_tok, wq.shape[1]), F32)
        for place in range(nx):
            total = total + mm(tok_all[place], wq[place * width : (place + 1) * width, :])
        queries.append(total)

    def inside(head):
        query = queries[0][:, head * size : (head + 1) * size]
        dots = dot3(query, keys[head], ((1,), (1,))) * incls[head]
        inner = dot3(dots, solves[head])
        intra[head] = inner[:, size:]
        eff[head] = query * jnp.exp(logs[head]) - inner[:, :size]

    def join(left, right):
        return by_map(left, right[:size]) + below(size, right[size:])

    def pairs(slots, count):
        levels = [[slots[j] for j in range(count)]]
        while len(levels[-1]) > 1:
            level = [part.astype(F32) for part in levels[-1]]
            levels.append([join(level[j], levels[-1][j + 1]) for j in range(0, len(level), 2)])
        return levels

    def pieces(levels, place):
        found = []
        for depth in reversed(range(len(levels) - 1)):
            step = 2 ** depth
            bit = (place // step) % 2 == 1
            chosen = levels[depth][0].astype(F32)
            for j in range(2, len(levels[depth]), 2):
                chosen = jnp.where(place // (2 * step) == j // 2, levels[depth][j].astype(F32), chosen)
            found.append(jnp.where(bit, chosen, unit))
        return found

    z_copies = ring(
        gz, z, nz, z_send, z_recv, (z_right, z_left),
        [ask, functools.partial(inside, 0), functools.partial(inside, 1)][: nz // 2],
    )
    if nz // 2 < 3:
        for late_work in [ask, functools.partial(inside, 0), functools.partial(inside, 1)][nz // 2 :]:
            late_work()
    levels = pairs(gz, nz)
    gy[y] = levels[-1][0].astype(WIRE)
    prefix = []

    def before_here():
        found = pieces(levels, z)
        total = found[0]
        for part in found[1:]:
            total = dot3(total, part[:size]) + below(size, part[size:])
        prefix.append(total)

    y_copies = ring(gy, y, ny, y_send, y_recv, (y_right, y_left), [before_here])
    found = pieces(pairs(gy, ny), y)
    state = found[0][size:]
    for part in found[1:] + prefix:
        state = dot3(state, part[:size]) + part[size:]
    chip = state
    second = dot3(chip, early[:size]) + early[size:]
    st_send[...] = jnp.where(first_core, second, chip)
    give = send(st_send, st_recv, core_send.at[1], core_recv.at[1], partner)
    give.start()
    kept = jnp.where(first_core, chip, second)
    loads[6].wait()
    loads[7].wait()
    give.wait_recv()
    got = st_recv[...]
    states = [jnp.where(first_core, kept, got), jnp.where(first_core, got, kept)]
    gain = gain_ref[...]
    for head in heads:
        o = intra[head] + dot3(eff[head], states[head], ((1,), (1,)))
        scale = lax.rsqrt(jnp.mean(o * o, -1, keepdims=True) + 1e-06)
        norm_all[x, :, head * size : (head + 1) * size] = (o * scale * gain).astype(BF16)

    result = [jnp.zeros((n_tok, out_cols), F32)]

    def finish(place, block):
        if block is None:
            for copy in out_copies:
                copy.wait_recv()
            block = norm_all[x]
        result[0] = result[0] + mm(block, wo_all[place])

    n_copies = x_gather(norm_all.at[x], norm_all, n_send, n_recv, finish)
    out_ref[...] = result[0].astype(BF16)
    for copy in tok_copies + out_copies + z_copies + y_copies + [swap, give] + n_copies:
        copy.wait_send()


def shards(ny, nz, nx, tokens, w_query, w_key, w_value, gate_codes, beta_codes, norm_gain, w_out):
    n_tok, width = tokens.shape
    size = norm_gain.shape[0]
    here = w_query.shape[1]
    hbm = pl.BlockSpec(memory_space=pltpu.HBM)
    chunks = 4
    dma = pltpu.SemaphoreType.DMA
    return pl.pallas_call(
        functools.partial(kernel, nx, ny, nz),
        out_shape=jax.ShapeDtypeStruct((n_tok, w_out.shape[1] // nx), BF16),
        in_specs=[hbm] * 8,
        out_specs=pl.BlockSpec(memory_space=pltpu.VMEM),
        scratch_shapes=[
            pltpu.VMEM((nx, n_tok, width), BF16),
            pltpu.VMEM(w_query.shape, BF16),
            pltpu.VMEM(w_key.shape, BF16),
            pltpu.VMEM(w_value.shape, BF16),
            pltpu.VMEM((nx, here, w_out.shape[1] // nx), BF16),
            pltpu.VMEM((2, n_tok), jnp.int32),
            pltpu.VMEM((2, n_tok), jnp.int32),
            pltpu.VMEM((1, size), F32),
            pltpu.VMEM((2 * size, size), F32),
            pltpu.VMEM((2 * size, size), F32),
            pltpu.VMEM((nz, 2 * size, size), WIRE),
            pltpu.VMEM((ny, 2 * size, size), WIRE),
            pltpu.VMEM((size, size), F32),
            pltpu.VMEM((size, size), F32),
            pltpu.VMEM((nx, n_tok, here), BF16),
            pltpu.VMEM((2, n_tok, size), F32),
            pltpu.VMEM((2, n_tok, size), F32),
            dma((8,)), dma((4, 2)), dma((4, 2)), dma((nx - 1,)), dma((nx - 1,)), dma((4, 2)), dma((4, 2)),
            dma((2,)), dma((2,)), dma((2, nz, chunks)), dma((2, nz, chunks)), dma((2, ny, chunks)),
            dma((2, ny, chunks)),
        ],
        compiler_params=pltpu.CompilerParams(
            collective_id=0, has_side_effects=True, vmem_limit_bytes=67043328
        ),
    )(tokens, w_query, w_key, w_value, gate_codes.T, beta_codes.T, norm_gain.reshape(1, size), w_out)


def solution(mesh):
    chips = mesh.shape["seq"] // 2
    nz = 1
    while nz * nz < chips:
        nz *= 2
    return jax.shard_map(
        functools.partial(shards, chips // nz, nz, mesh.shape["head"]),
        mesh=mesh,
        in_specs=(
            P("seq", "head"), P(None, "head"), P(None, "head"), P(None, "head"),
            P("seq", "head"), P("seq", "head"), P(), P("head", None),
        ),
        out_specs=P("seq", "head"),
        check_vma=False,
    )
```

```python
import functools
import jax
import jax.numpy as jnp
from jax import lax
from jax.experimental import pallas as pl
from jax.experimental.pallas import tpu as pltpu
from jax.sharding import PartitionSpec as P

MESH = pl.DeviceIdType.MESH
WIRE = jnp.bfloat16
F32 = jnp.float32
BF16 = jnp.bfloat16


def mm(a, b, dims=((1,), (0,))):
    return lax.dot_general(a, b, (dims, ((), ())), preferred_element_type=F32)


def halves(a):
    high = a.astype(BF16)
    return high, (a - high.astype(F32)).astype(BF16)


def dot3(a, b, dims=((1,), (0,))):
    a_high, a_low = halves(a)
    b_high, b_low = halves(b)
    return mm(a_high, b_high, dims) + (mm(a_high, b_low, dims) + mm(a_low, b_high, dims))


def dot2(a, b):
    a_high, a_low = halves(a)
    return mm(a_high, b) + mm(a_low, b)


def by_map(a, b):
    return dot2(a, b) if b.dtype == BF16 else dot3(a, b)


def below(top, rows):
    return jnp.concatenate([jnp.zeros((top, rows.shape[1]), F32), rows.astype(F32)], axis=0)


def unit_inverse(low, rows, cols):
    size = low.shape[0]
    eye = (rows == cols).astype(F32)
    base = jnp.where(rows // 8 == cols // 8, low, 0.0)
    square = dot3(base, base)
    fourth = dot3(square, square)
    result = dot3(dot3(eye - base, eye + square), eye + fourth)
    width = 8
    while width < size:
        mask = (rows // (2 * width) == cols // (2 * width)) & (rows // width > cols // width)
        corner = jnp.where(mask, low, 0.0)
        result = result - dot3(dot3(result, corner), result)
        width *= 2
    return result


def kernel(
    nx, ny, nz,
    tok_hbm, wq_hbm, wk_hbm, wv_hbm, gate_hbm, beta_hbm, gain_hbm, wo_hbm,
    out_ref,
    tok_all, wq, wk, wv, wo_all, gate_ref, beta_ref, gain_ref, ex_send, ex_recv, gz, gy, st_send, st_recv,
    norm_all, eff, intra,
    load_sem, x_send, x_recv, wo_send, wo_recv, n_send, n_recv, core_send, core_recv,
    z_send, z_recv, y_send, y_recv,
):
    index = lax.axis_index("seq")
    x = lax.axis_index("head")
    core = index % 2
    z = (index // 2) % nz
    y = index // (2 * nz)
    size = gain_ref.shape[1]
    n_tok, width = tok_hbm.shape
    out_cols = out_ref.shape[1]

    def at(to_y, to_z, to_core, to_x):
        return ((to_y * nz + to_z) * 2 + to_core, to_x)

    x_right, x_left = at(y, z, core, (x + 1) % nx), at(y, z, core, (x + nx - 1) % nx)

    def z_to(d):
        return at(y, (z + d + nz) % nz, core, x)

    def y_to(d):
        return at((y + d + ny) % ny, z, core, x)

    partner = at(y, z, 1 - core, x)

    friends = [at(y, z, core, (x + d) % nx) for d in range(1, nx)]
    friends += [partner]
    for count, toward in ((nz, z_to), (ny, y_to)):
        steps = {d % count for d in ((1, -1, 2, -2) if count == 8 else (1, -1))} - {0}
        friends += [toward(d) for d in sorted(steps)]
    barrier = pltpu.get_barrier_semaphore()
    for friend in friends:
        pl.semaphore_signal(barrier, inc=1, device_id=friend, device_id_type=MESH)

    own_cols = pl.ds(pl.multiple_of(x * out_cols, 128), out_cols)
    loads = [
        pltpu.make_async_copy(source, target, load_sem.at[i])
        for i, (source, target) in enumerate(
            (
                (tok_hbm, tok_all.at[x]), (gate_hbm, gate_ref), (beta_hbm, beta_ref), (wk_hbm, wk),
                (wv_hbm, wv), (wq_hbm, wq), (gain_hbm, gain_ref), (wo_hbm.at[:, own_cols], wo_all.at[x]),
            )
        )
    ]
    for load in loads:
        load.start()
    pl.semaphore_wait(barrier, len(friends))

    def send(source, target, s_sem, r_sem, to):
        return pltpu.make_async_remote_copy(
            src_ref=source, dst_ref=target, send_sem=s_sem, recv_sem=r_sem,
            device_id=to, device_id_type=MESH,
        )

    def x_gather(own, slots, s_sems, r_sems, use):
        half = own.shape[0] // 2
        before, after, across = (x + nx - 1) % nx, (x + 1) % nx, (x + 2) % nx
        first, second = [], []
        for k, part in enumerate((0, half)):
            other = half - part
            first.append(
                send(own.at[pl.ds(part, half)], slots.at[x, pl.ds(part, half)], s_sems.at[0, k], r_sems.at[0, k], x_right)
            )
            second.append(
                send(own.at[pl.ds(other, half)], slots.at[x, pl.ds(other, half)], s_sems.at[1, k], r_sems.at[1, k], x_left)
            )
            first[k].start()
            second[k].start()
        use(x, None)
        first[0].wait_recv()
        top = slots.at[before, pl.ds(0, half)]
        third = send(top, top, s_sems.at[2, 0], r_sems.at[2, 0], x_right)
        third.start()
        second[0].wait_recv()
        low = slots.at[after, pl.ds(half, half)]
        fourth = send(low, low, s_sems.at[3, 0], r_sems.at[3, 0], x_left)
        fourth.start()
        first[1].wait_recv()
        use(before, slots[before])
        second[1].wait_recv()
        use(after, slots[after])
        third.wait_recv()
        fourth.wait_recv()
        use(across, slots[across])
        return first + second + [third, fourth]

    rows = lax.broadcasted_iota(jnp.int32, (n_tok, n_tok), 0)
    cols = lax.broadcasted_iota(jnp.int32, (n_tok, n_tok), 1)
    lower = rows >= cols
    r2 = lax.broadcasted_iota(jnp.int32, (2 * size, size), 0)
    c2 = lax.broadcasted_iota(jnp.int32, (2 * size, size), 1)
    unit = (r2 == c2).astype(F32)
    heads = range(2)
    logs, incls, betas, lasts = [], [], [], []

    def gates():
        loads[1].wait()
        loads[2].wait()
        ones_up = (rows <= cols).astype(BF16)
        for head in heads:
            code = -gate_ref[head : head + 1, :].astype(F32) / 2097152.0
            beta = beta_ref[head : head + 1, :].astype(F32) / 256.0
            spread = jnp.broadcast_to(code, (n_tok, n_tok))
            c_high, c_low = halves(spread)
            c_last = (spread - c_high.astype(F32) - c_low.astype(F32)).astype(BF16)
            across = mm(c_high, ones_up) + (mm(c_low, ones_up) + mm(c_last, ones_up))
            log = across.T
            gaps = log - across
            logs.append(log)
            incls.append(jnp.where(lower, jnp.exp(jnp.where(lower, gaps, 0.0)), 0.0))
            betas.append(jnp.broadcast_to(beta, (n_tok, n_tok)).T)
            lasts.append(across[0:1, n_tok - 1 : n_tok])

    sums = [jnp.zeros((n_tok, wq.shape[1]), F32) for _ in range(2)]

    def project(place, block):
        if block is None:
            gates()
            loads[0].wait()
            loads[3].wait()
            loads[4].wait()
            block = tok_all[x]
        part = pl.ds(pl.multiple_of(place * width, 128), width)
        for i, weight in enumerate((wk, wv)):
            sums[i] = sums[i] + mm(block, weight[part, :])

    tok_copies = x_gather(tok_hbm, tok_all, x_send, x_recv, project)

    out_copies = []
    for d in range(1, nx):
        there = (x + d) % nx
        there_cols = pl.ds(pl.multiple_of(there * out_cols, 128), out_cols)
        out_copies.append(
            send(wo_hbm.at[:, there_cols], wo_all.at[x], wo_send.at[d - 1], wo_recv.at[d - 1],
                 at(y, z, core, there))
        )
    for copy in out_copies:
        copy.start()

    maps, keys, solves = [], [], []
    for head in heads:
        cut = slice(head * size, (head + 1) * size)
        key, value = (s[:, cut] for s in sums)
        key = key * lax.rsqrt(jnp.sum(key * key, -1, keepdims=True) + 1e-06)
        beta, log, last = betas[head], logs[head], lasts[head]
        low = jnp.where(rows > cols, beta * dot3(key, key, ((1,), (1,))) * incls[head], 0.0)
        inverse = unit_inverse(low, rows, cols)
        right = jnp.concatenate([beta * key * jnp.exp(log), beta * value], axis=1)
        solved = dot3(inverse, right)
        tail = key * jnp.exp(last - log)
        signed = jnp.concatenate([-solved[:, :size], solved[:, size:]], axis=1)
        moved = dot3(signed, tail, ((0,), (0,)))
        maps.append(moved + jnp.where(r2 == c2, jnp.exp(last), 0.0))
        keys.append(key)
        solves.append(solved)

    first_core = core == 0
    ex_send[...] = jnp.where(first_core, maps[1], maps[0])
    swap = send(ex_send, ex_recv, core_send.at[0], core_recv.at[0], partner)
    swap.start()
    mine = jnp.where(first_core, maps[0], maps[1])
    swap.wait_recv()
    other = ex_recv[...]
    early = jnp.where(first_core, mine, other)
    late = jnp.where(first_core, other, mine)
    gz[z] = (dot3(early, late[:size]) + below(size, late[size:])).astype(WIRE)

    def ring_of_eight(slots, place, s_sems, r_sems, to, fill):
        chunks = r_sems.shape[2]
        rows_each = slots.shape[1] // chunks
        copies = {}

        def go(way, distance, chunk, hops):
            sign = 1 - 2 * way
            slot = (place - sign * (distance - hops) + 8) % 8
            piece = slots.at[slot, pl.ds(chunk * rows_each, rows_each)]
            copy = send(
                piece, piece, s_sems.at[way, distance - 1, chunk], r_sems.at[way, distance - 1, chunk], to(sign * hops)
            )
            copy.start()
            copies[way, distance, chunk] = copy

        order = list(range(chunks))
        turns = (order, order[::-1])
        for distance in (2, 1):
            for k in order:
                for way in range(2):
                    go(way, distance, turns[way][k], distance)
        fill[0]()
        for k in order:
            for way in range(2):
                chunk = turns[way][k]
                copies[way, 2, chunk].wait_recv()
                if k < chunks // 2:
                    go(way, 4, chunk, 2)
                go(way, 3, chunk, 1)
        for work in fill[1:]:
            work()
        for (way, distance, chunk), copy in copies.items():
            if distance != 2:
                copy.wait_recv()
        return list(copies.values())

    def ring(slots, place, count, s_sems, r_sems, to, fill):
        if count == 8:
            return ring_of_eight(slots, place, s_sems, r_sems, to, fill)
        chunks = r_sems.shape[2]
        rows_each = slots.shape[1] // chunks
        far = count // 2
        sent = []
        waiting = {}
        for step in range(far):
            for chunk in range(chunks):
                for way in range(2):
                    if step == far - 1 and (chunk < chunks // 2) != (way == 0):
                        continue
                    if step:
                        waiting.pop((way, step - 1, chunk)).wait_recv()
                    slot = (place + count - step) % count if way == 0 else (place + step) % count
                    piece = slots.at[slot, pl.ds(chunk * rows_each, rows_each)]
                    copy = send(
                        piece, piece, s_sems.at[way, step, chunk], r_sems.at[way, step, chunk], to(1 - 2 * way)
                    )
                    copy.start()
                    sent.append(copy)
                    waiting[way, step, chunk] = copy
            if step < len(fill):
                fill[step]()
        for copy in waiting.values():
            copy.wait_recv()
        return sent

    queries = []

    def ask():
        loads[5].wait()
        total = jnp.zeros((n_tok, wq.shape[1]), F32)
        for place in range(nx):
            total = total + mm(tok_all[place], wq[place * width : (place + 1) * width, :])
        queries.append(total)

    def inside(head):
        query = queries[0][:, head * size : (head + 1) * size]
        dots = dot3(query, keys[head], ((1,), (1,))) * incls[head]
        inner = dot3(dots, solves[head])
        intra[head] = inner[:, size:]
        eff[head] = query * jnp.exp(logs[head]) - inner[:, :size]

    def join(left, right):
        return by_map(left, right[:size]) + below(size, right[size:])

    def pairs(slots, count):
        levels = [[slots[j] for j in range(count)]]
        while len(levels[-1]) > 1:
            level = [part.astype(F32) for part in levels[-1]]
            levels.append([join(level[j], levels[-1][j + 1]) for j in range(0, len(level), 2)])
        return levels

    def pieces(levels, place):
        found = []
        for depth in reversed(range(len(levels) - 1)):
            step = 2 ** depth
            bit = (place // step) % 2 == 1
            chosen = levels[depth][0].astype(F32)
            for j in range(2, len(levels[depth]), 2):
                chosen = jnp.where(place // (2 * step) == j // 2, levels[depth][j].astype(F32), chosen)
            found.append(jnp.where(bit, chosen, unit))
        return found

    def rest():
        for head in heads:
            inside(head)

    z_copies = ring(gz, z, nz, z_send, z_recv, z_to, [ask, rest])
    levels = pairs(gz, nz)
    gy[y] = levels[-1][0].astype(WIRE)
    prefix = []

    def before_here():
        found = pieces(levels, z)
        total = found[0]
        for part in found[1:]:
            total = dot3(total, part[:size]) + below(size, part[size:])
        prefix.append(total)

    y_copies = ring(gy, y, ny, y_send, y_recv, y_to, [before_here])
    found = pieces(pairs(gy, ny), y)
    state = found[0][size:]
    for part in found[1:] + prefix:
        state = dot3(state, part[:size]) + part[size:]
    chip = state
    second = dot3(chip, early[:size]) + early[size:]
    st_send[...] = jnp.where(first_core, second, chip)
    give = send(st_send, st_recv, core_send.at[1], core_recv.at[1], partner)
    give.start()
    kept = jnp.where(first_core, chip, second)
    loads[6].wait()
    loads[7].wait()
    give.wait_recv()
    got = st_recv[...]
    states = [jnp.where(first_core, kept, got), jnp.where(first_core, got, kept)]
    gain = gain_ref[...]
    for head in heads:
        o = intra[head] + dot3(eff[head], states[head], ((1,), (1,)))
        scale = lax.rsqrt(jnp.mean(o * o, -1, keepdims=True) + 1e-06)
        norm_all[x, :, head * size : (head + 1) * size] = (o * scale * gain).astype(BF16)

    result = [jnp.zeros((n_tok, out_cols), F32)]

    def finish(place, block):
        if block is None:
            for copy in out_copies:
                copy.wait_recv()
            block = norm_all[x]
        result[0] = result[0] + mm(block, wo_all[place])

    n_copies = x_gather(norm_all.at[x], norm_all, n_send, n_recv, finish)
    out_ref[...] = result[0].astype(BF16)
    for copy in tok_copies + out_copies + z_copies + y_copies + [swap, give] + n_copies:
        copy.wait_send()


def shards(ny, nz, nx, tokens, w_query, w_key, w_value, gate_codes, beta_codes, norm_gain, w_out):
    n_tok, width = tokens.shape
    size = norm_gain.shape[0]
    here = w_query.shape[1]
    hbm = pl.BlockSpec(memory_space=pltpu.HBM)
    chunks = 2
    dma = pltpu.SemaphoreType.DMA
    return pl.pallas_call(
        functools.partial(kernel, nx, ny, nz),
        out_shape=jax.ShapeDtypeStruct((n_tok, w_out.shape[1] // nx), BF16),
        in_specs=[hbm] * 8,
        out_specs=pl.BlockSpec(memory_space=pltpu.VMEM),
        scratch_shapes=[
            pltpu.VMEM((nx, n_tok, width), BF16),
            pltpu.VMEM(w_query.shape, BF16),
            pltpu.VMEM(w_key.shape, BF16),
            pltpu.VMEM(w_value.shape, BF16),
            pltpu.VMEM((nx, here, w_out.shape[1] // nx), BF16),
            pltpu.VMEM((2, n_tok), jnp.int32),
            pltpu.VMEM((2, n_tok), jnp.int32),
            pltpu.VMEM((1, size), F32),
            pltpu.VMEM((2 * size, size), F32),
            pltpu.VMEM((2 * size, size), F32),
            pltpu.VMEM((nz, 2 * size, size), WIRE),
            pltpu.VMEM((ny, 2 * size, size), WIRE),
            pltpu.VMEM((size, size), F32),
            pltpu.VMEM((size, size), F32),
            pltpu.VMEM((nx, n_tok, here), BF16),
            pltpu.VMEM((2, n_tok, size), F32),
            pltpu.VMEM((2, n_tok, size), F32),
            dma((8,)), dma((4, 2)), dma((4, 2)), dma((nx - 1,)), dma((nx - 1,)), dma((4, 2)), dma((4, 2)),
            dma((2,)), dma((2,)), dma((2, nz, chunks)), dma((2, nz, chunks)), dma((2, ny, chunks)),
            dma((2, ny, chunks)),
        ],
        compiler_params=pltpu.CompilerParams(
            collective_id=0, has_side_effects=True, vmem_limit_bytes=67043328
        ),
    )(tokens, w_query, w_key, w_value, gate_codes.T, beta_codes.T, norm_gain.reshape(1, size), w_out)


def along_z(chips):
    nz = 1
    while nz * nz < chips:
        nz *= 2
    return nz


def solution(mesh):
    chips = mesh.shape["seq"] // 2
    nz = along_z(chips)
    return jax.shard_map(
        functools.partial(shards, chips // nz, nz, mesh.shape["head"]),
        mesh=mesh,
        in_specs=(
            P("seq", "head"), P(None, "head"), P(None, "head"), P(None, "head"),
            P("seq", "head"), P("seq", "head"), P(), P("head", None),
        ),
        out_specs=P("seq", "head"),
        check_vma=False,
    )
```

```python
import functools
import jax
import jax.numpy as jnp
from jax import lax
from jax.experimental import pallas as pl
from jax.experimental.pallas import tpu as pltpu
from jax.sharding import PartitionSpec as P

MESH = pl.DeviceIdType.MESH
WIRE = jnp.bfloat16
F32 = jnp.float32
BF16 = jnp.bfloat16


def mm(a, b, dims=((1,), (0,))):
    return lax.dot_general(a, b, (dims, ((), ())), preferred_element_type=F32)


def halves(a):
    high = a.astype(BF16)
    return high, (a - high.astype(F32)).astype(BF16)


def dot3(a, b, dims=((1,), (0,))):
    a_high, a_low = halves(a)
    b_high, b_low = halves(b)
    free = 1 - dims[1][0]
    count = b.shape[free]
    both = mm(a_high, jnp.concatenate([b_high, b_low], axis=free), dims)
    return both[:, :count] + (both[:, count:] + mm(a_low, b_high, dims))


def dot2(a, b):
    a_high, a_low = halves(a)
    return mm(a_high, b) + mm(a_low, b)


def by_map(a, b):
    return dot2(a, b) if b.dtype == BF16 else dot3(a, b)


def below(top, rows):
    return jnp.concatenate([jnp.zeros((top, rows.shape[1]), F32), rows.astype(F32)], axis=0)


def unit_inverse(low, rows, cols):
    size = low.shape[0]
    eye = (rows == cols).astype(F32)
    base = jnp.where(rows // 8 == cols // 8, low, 0.0)
    square = dot3(base, base)
    fourth = dot3(square, square)
    result = dot3(dot3(eye - base, eye + square), eye + fourth)
    width = 8
    while width < size:
        mask = (rows // (2 * width) == cols // (2 * width)) & (rows // width > cols // width)
        corner = jnp.where(mask, low, 0.0)
        result = result - dot3(dot3(result, corner), result)
        width *= 2
    return result


def kernel(
    nx, ny, nz,
    tok_hbm, wq_hbm, wk_hbm, wv_hbm, gate_hbm, beta_hbm, gain_hbm, wo_hbm,
    out_ref,
    tok_all, wq, wk, wv, wo_all, gate_ref, beta_ref, gain_ref, ex_send, ex_recv, gz, gy, st_send, st_recv,
    norm_all, eff, intra,
    load_sem, x_send, x_recv, wo_send, wo_recv, n_send, n_recv, core_send, core_recv,
    z_send, z_recv, y_send, y_recv,
):
    index = lax.axis_index("seq")
    x = lax.axis_index("head")
    core = index % 2
    z = (index // 2) % nz
    y = index // (2 * nz)
    size = gain_ref.shape[1]
    n_tok, width = tok_hbm.shape
    out_cols = out_ref.shape[1]

    def at(to_y, to_z, to_core, to_x):
        return ((to_y * nz + to_z) * 2 + to_core, to_x)

    x_right, x_left = at(y, z, core, (x + 1) % nx), at(y, z, core, (x + nx - 1) % nx)

    def z_to(d):
        return at(y, (z + d + nz) % nz, core, x)

    def y_to(d):
        return at((y + d + ny) % ny, z, core, x)

    partner = at(y, z, 1 - core, x)

    friends = [at(y, z, core, (x + d) % nx) for d in range(1, nx)]
    friends += [partner]
    for count, toward in ((nz, z_to), (ny, y_to)):
        steps = {d % count for d in ((1, -1, 2, -2) if count == 8 else (1, -1))} - {0}
        friends += [toward(d) for d in sorted(steps)]
    gy[...] = jnp.zeros(gy.shape, WIRE)
    barrier = pltpu.get_barrier_semaphore()
    for friend in friends:
        pl.semaphore_signal(barrier, inc=1, device_id=friend, device_id_type=MESH)

    own_cols = pl.ds(pl.multiple_of(x * out_cols, 128), out_cols)
    loads = [
        pltpu.make_async_copy(source, target, load_sem.at[i])
        for i, (source, target) in enumerate(
            (
                (tok_hbm, tok_all.at[x]), (gate_hbm, gate_ref), (beta_hbm, beta_ref), (wk_hbm, wk),
                (wv_hbm, wv), (wq_hbm, wq), (gain_hbm, gain_ref), (wo_hbm.at[:, own_cols], wo_all.at[x]),
            )
        )
    ]
    for load in loads:
        load.start()
    pl.semaphore_wait(barrier, len(friends))

    def send(source, target, s_sem, r_sem, to):
        return pltpu.make_async_remote_copy(
            src_ref=source, dst_ref=target, send_sem=s_sem, recv_sem=r_sem,
            device_id=to, device_id_type=MESH,
        )

    def x_gather(own, slots, s_sems, r_sems, use):
        half = own.shape[0] // 2
        before, after, across = (x + nx - 1) % nx, (x + 1) % nx, (x + 2) % nx
        first, second = [], []
        for k, part in enumerate((0, half)):
            other = half - part
            first.append(
                send(own.at[pl.ds(part, half)], slots.at[x, pl.ds(part, half)], s_sems.at[0, k], r_sems.at[0, k], x_right)
            )
            second.append(
                send(own.at[pl.ds(other, half)], slots.at[x, pl.ds(other, half)], s_sems.at[1, k], r_sems.at[1, k], x_left)
            )
            first[k].start()
            second[k].start()
        use(x, None)
        first[0].wait_recv()
        top = slots.at[before, pl.ds(0, half)]
        third = send(top, top, s_sems.at[2, 0], r_sems.at[2, 0], x_right)
        third.start()
        second[0].wait_recv()
        low = slots.at[after, pl.ds(half, half)]
        fourth = send(low, low, s_sems.at[3, 0], r_sems.at[3, 0], x_left)
        fourth.start()
        first[1].wait_recv()
        use(before, slots[before])
        second[1].wait_recv()
        use(after, slots[after])
        third.wait_recv()
        fourth.wait_recv()
        use(across, slots[across])
        return first + second + [third, fourth]

    rows = lax.broadcasted_iota(jnp.int32, (n_tok, n_tok), 0)
    cols = lax.broadcasted_iota(jnp.int32, (n_tok, n_tok), 1)
    lower = rows >= cols
    r2 = lax.broadcasted_iota(jnp.int32, (2 * size, size), 0)
    c2 = lax.broadcasted_iota(jnp.int32, (2 * size, size), 1)
    unit = (r2 == c2).astype(F32)
    heads = range(2)
    logs, incls, betas, lasts = [], [], [], []

    def gates():
        loads[1].wait()
        loads[2].wait()
        ones_up = (rows <= cols).astype(BF16)
        for head in heads:
            code = -gate_ref[head : head + 1, :].astype(F32) / 2097152.0
            beta = beta_ref[head : head + 1, :].astype(F32) / 256.0
            spread = jnp.broadcast_to(code, (n_tok, n_tok))
            c_high, c_low = halves(spread)
            c_last = (spread - c_high.astype(F32) - c_low.astype(F32)).astype(BF16)
            across = mm(c_high, ones_up) + (mm(c_low, ones_up) + mm(c_last, ones_up))
            log = across.T
            gaps = log - across
            logs.append(log)
            incls.append(jnp.where(lower, jnp.exp(jnp.where(lower, gaps, 0.0)), 0.0))
            betas.append(jnp.broadcast_to(beta, (n_tok, n_tok)).T)
            lasts.append(across[0:1, n_tok - 1 : n_tok])

    sums = [jnp.zeros((n_tok, wq.shape[1]), F32) for _ in range(2)]

    def project(place, block):
        if block is None:
            gates()
            loads[0].wait()
            loads[3].wait()
            loads[4].wait()
            block = tok_all[x]
        part = pl.ds(pl.multiple_of(place * width, 128), width)
        for i, weight in enumerate((wk, wv)):
            sums[i] = sums[i] + mm(block, weight[part, :])

    tok_copies = x_gather(tok_hbm, tok_all, x_send, x_recv, project)

    out_copies = []
    for d in range(1, nx):
        there = (x + d) % nx
        there_cols = pl.ds(pl.multiple_of(there * out_cols, 128), out_cols)
        out_copies.append(
            send(wo_hbm.at[:, there_cols], wo_all.at[x], wo_send.at[d - 1], wo_recv.at[d - 1],
                 at(y, z, core, there))
        )
    for copy in out_copies:
        copy.start()

    maps, keys, solves = [], [], []
    for head in heads:
        cut = slice(head * size, (head + 1) * size)
        key, value = (s[:, cut] for s in sums)
        key = key * lax.rsqrt(jnp.sum(key * key, -1, keepdims=True) + 1e-06)
        beta, log, last = betas[head], logs[head], lasts[head]
        low = jnp.where(rows > cols, beta * dot3(key, key, ((1,), (1,))) * incls[head], 0.0)
        inverse = unit_inverse(low, rows, cols)
        right = jnp.concatenate([beta * key * jnp.exp(log), beta * value], axis=1)
        solved = dot3(inverse, right)
        tail = key * jnp.exp(last - log)
        signed = jnp.concatenate([-solved[:, :size], solved[:, size:]], axis=1)
        moved = dot3(signed, tail, ((0,), (0,)))
        maps.append(moved + jnp.where(r2 == c2, jnp.exp(last), 0.0))
        keys.append(key)
        solves.append(solved)

    first_core = core == 0
    ex_send[...] = jnp.where(first_core, maps[1], maps[0])
    swap = send(ex_send, ex_recv, core_send.at[0], core_recv.at[0], partner)
    swap.start()
    mine = jnp.where(first_core, maps[0], maps[1])
    swap.wait_recv()
    other = ex_recv[...]
    early = jnp.where(first_core, mine, other)
    late = jnp.where(first_core, other, mine)
    gz[z] = (dot3(early, late[:size]) + below(size, late[size:])).astype(WIRE)

    def ring_of_eight(slots, place, s_sems, r_sems, to, fill, earlier_only):
        chunks = r_sems.shape[2]
        rows_each = slots.shape[1] // chunks
        copies = {}

        def wanted(way, distance, source, act):
            if earlier_only:
                limit = 8 - distance if way == 0 else (1, 4, 3, 4)[distance - 1]
                pl.when(source < limit)(act)
            else:
                act()

        def go(way, distance, chunk, hops):
            sign = 1 - 2 * way
            slot = (place - sign * (distance - hops) + 8) % 8
            piece = slots.at[slot, pl.ds(chunk * rows_each, rows_each)]
            copy = send(
                piece, piece, s_sems.at[way, distance - 1, chunk], r_sems.at[way, distance - 1, chunk], to(sign * hops)
            )
            wanted(way, distance, slot, copy.start)
            copies[way, distance, chunk] = copy, slot

        def arrive(way, distance, chunk):
            source = (place - (1 - 2 * way) * distance + 8) % 8
            wanted(way, distance, source, copies[way, distance, chunk][0].wait_recv)

        order = list(range(chunks))
        turns = (order, order[::-1])
        for distance in (2, 1):
            for k in order:
                for way in range(2):
                    go(way, distance, turns[way][k], distance)
        fill[0]()
        for k in order:
            for way in range(2):
                chunk = turns[way][k]
                arrive(way, 2, chunk)
                if way == 1 if earlier_only else k < chunks // 2:
                    go(way, 4, chunk, 2)
                go(way, 3, chunk, 1)
        for work in fill[1:]:
            work()
        for way, distance, chunk in copies:
            if distance != 2:
                arrive(way, distance, chunk)

        def left(way, distance, copy, slot):
            wanted(way, distance, slot, copy.wait_send)

        return [functools.partial(left, way, distance, *copy) for (way, distance, _), copy in copies.items()]

    def ring(slots, place, count, s_sems, r_sems, to, fill, earlier_only=False):
        if count == 8:
            return ring_of_eight(slots, place, s_sems, r_sems, to, fill, earlier_only)
        chunks = r_sems.shape[2]
        rows_each = slots.shape[1] // chunks
        far = count // 2
        sent = []
        waiting = {}
        for step in range(far):
            for chunk in range(chunks):
                for way in range(2):
                    if step == far - 1 and (chunk < chunks // 2) != (way == 0):
                        continue
                    if step:
                        waiting.pop((way, step - 1, chunk)).wait_recv()
                    slot = (place + count - step) % count if way == 0 else (place + step) % count
                    piece = slots.at[slot, pl.ds(chunk * rows_each, rows_each)]
                    copy = send(
                        piece, piece, s_sems.at[way, step, chunk], r_sems.at[way, step, chunk], to(1 - 2 * way)
                    )
                    copy.start()
                    sent.append(copy)
                    waiting[way, step, chunk] = copy
            if step < len(fill):
                fill[step]()
        for work in fill[far:]:
            work()
        for copy in waiting.values():
            copy.wait_recv()
        return [copy.wait_send for copy in sent]

    queries = []

    def ask():
        loads[5].wait()
        total = jnp.zeros((n_tok, wq.shape[1]), F32)
        for place in range(nx):
            total = total + mm(tok_all[place], wq[place * width : (place + 1) * width, :])
        queries.append(total)

    def inside(head):
        query = queries[0][:, head * size : (head + 1) * size]
        dots = dot3(query, keys[head], ((1,), (1,))) * incls[head]
        inner = dot3(dots, solves[head])
        intra[head] = inner[:, size:]
        eff[head] = query * jnp.exp(logs[head]) - inner[:, :size]

    def join(left, right):
        return by_map(left, right[:size]) + below(size, right[size:])

    def pairs(slots, count):
        levels = [[slots[j] for j in range(count)]]
        while len(levels[-1]) > 1:
            level = [part.astype(F32) for part in levels[-1]]
            levels.append([join(level[j], levels[-1][j + 1]) for j in range(0, len(level), 2)])
        return levels

    def pieces(levels, place):
        found = []
        for depth in reversed(range(len(levels) - 1)):
            step = 2 ** depth
            bit = (place // step) % 2 == 1
            chosen = levels[depth][0].astype(F32)
            for j in range(2, len(levels[depth]), 2):
                chosen = jnp.where(place // (2 * step) == j // 2, levels[depth][j].astype(F32), chosen)
            found.append(jnp.where(bit, chosen, unit))
        return found

    def rest():
        for head in heads:
            inside(head)

    z_copies = ring(gz, z, nz, z_send, z_recv, z_to, [ask, rest])
    levels = pairs(gz, nz)
    gy[y] = levels[-1][0].astype(WIRE)
    prefix = []

    def before_here():
        found = pieces(levels, z)
        total = found[0]
        for part in found[1:]:
            total = dot3(total, part[:size]) + below(size, part[size:])
        prefix.append(total)

    y_copies = ring(gy, y, ny, y_send, y_recv, y_to, [before_here], True)
    found = pieces(pairs(gy, ny), y)
    state = found[0][size:]
    for part in found[1:] + prefix:
        state = dot3(state, part[:size]) + part[size:]
    chip = state
    second = dot3(chip, early[:size]) + early[size:]
    st_send[...] = jnp.where(first_core, second, chip)
    give = send(st_send, st_recv, core_send.at[1], core_recv.at[1], partner)
    give.start()
    kept = jnp.where(first_core, chip, second)
    loads[6].wait()
    loads[7].wait()
    give.wait_recv()
    got = st_recv[...]
    states = [jnp.where(first_core, kept, got), jnp.where(first_core, got, kept)]
    gain = gain_ref[...]
    for head in heads:
        o = intra[head] + dot3(eff[head], states[head], ((1,), (1,)))
        scale = lax.rsqrt(jnp.mean(o * o, -1, keepdims=True) + 1e-06)
        norm_all[x, :, head * size : (head + 1) * size] = (o * scale * gain).astype(BF16)

    result = [jnp.zeros((n_tok, out_cols), F32)]

    def finish(place, block):
        if block is None:
            for copy in out_copies:
                copy.wait_recv()
            block = norm_all[x]
        result[0] = result[0] + mm(block, wo_all[place])

    n_copies = x_gather(norm_all.at[x], norm_all, n_send, n_recv, finish)
    out_ref[...] = result[0].astype(BF16)
    for copy in tok_copies + out_copies + [swap, give] + n_copies:
        copy.wait_send()
    for finished in z_copies + y_copies:
        finished()


def shards(ny, nz, nx, tokens, w_query, w_key, w_value, gate_codes, beta_codes, norm_gain, w_out):
    n_tok, width = tokens.shape
    size = norm_gain.shape[0]
    here = w_query.shape[1]
    hbm = pl.BlockSpec(memory_space=pltpu.HBM)
    chunks = 2
    dma = pltpu.SemaphoreType.DMA
    return pl.pallas_call(
        functools.partial(kernel, nx, ny, nz),
        out_shape=jax.ShapeDtypeStruct((n_tok, w_out.shape[1] // nx), BF16),
        in_specs=[hbm] * 8,
        out_specs=pl.BlockSpec(memory_space=pltpu.VMEM),
        scratch_shapes=[
            pltpu.VMEM((nx, n_tok, width), BF16),
            pltpu.VMEM(w_query.shape, BF16),
            pltpu.VMEM(w_key.shape, BF16),
            pltpu.VMEM(w_value.shape, BF16),
            pltpu.VMEM((nx, here, w_out.shape[1] // nx), BF16),
            pltpu.VMEM((2, n_tok), jnp.int32),
            pltpu.VMEM((2, n_tok), jnp.int32),
            pltpu.VMEM((1, size), F32),
            pltpu.VMEM((2 * size, size), F32),
            pltpu.VMEM((2 * size, size), F32),
            pltpu.VMEM((nz, 2 * size, size), WIRE),
            pltpu.VMEM((ny, 2 * size, size), WIRE),
            pltpu.VMEM((size, size), F32),
            pltpu.VMEM((size, size), F32),
            pltpu.VMEM((nx, n_tok, here), BF16),
            pltpu.VMEM((2, n_tok, size), F32),
            pltpu.VMEM((2, n_tok, size), F32),
            dma((8,)), dma((4, 2)), dma((4, 2)), dma((nx - 1,)), dma((nx - 1,)), dma((4, 2)), dma((4, 2)),
            dma((2,)), dma((2,)), dma((2, nz, chunks)), dma((2, nz, chunks)), dma((2, ny, chunks)),
            dma((2, ny, chunks)),
        ],
        compiler_params=pltpu.CompilerParams(
            collective_id=0, has_side_effects=True, vmem_limit_bytes=67043328
        ),
    )(tokens, w_query, w_key, w_value, gate_codes.T, beta_codes.T, norm_gain.reshape(1, size), w_out)


def along_z(chips):
    nz = 1
    while nz * nz < chips:
        nz *= 2
    return nz


def solution(mesh):
    chips = mesh.shape["seq"] // 2
    nz = along_z(chips)
    return jax.shard_map(
        functools.partial(shards, chips // nz, nz, mesh.shape["head"]),
        mesh=mesh,
        in_specs=(
            P("seq", "head"), P(None, "head"), P(None, "head"), P(None, "head"),
            P("seq", "head"), P("seq", "head"), P(), P("head", None),
        ),
        out_specs=P("seq", "head"),
        check_vma=False,
    )
```

```python
import functools
import jax
import jax.numpy as jnp
from jax import lax
from jax.experimental import pallas as pl
from jax.experimental.pallas import tpu as pltpu
from jax.sharding import PartitionSpec as P

MESH = pl.DeviceIdType.MESH
WIRE = jnp.bfloat16
F32 = jnp.float32
BF16 = jnp.bfloat16


def mm(a, b, dims=((1,), (0,))):
    return lax.dot_general(a, b, (dims, ((), ())), preferred_element_type=F32)


def halves(a):
    high = a.astype(BF16)
    return high, (a - high.astype(F32)).astype(BF16)


def dot3(a, b, dims=((1,), (0,))):
    a_high, a_low = halves(a)
    b_high, b_low = halves(b)
    free = 1 - dims[1][0]
    count = b.shape[free]
    both = mm(a_high, jnp.concatenate([b_high, b_low], axis=free), dims)
    return both[:, :count] + (both[:, count:] + mm(a_low, b_high, dims))


def dot2(a, b):
    a_high, a_low = halves(a)
    return mm(a_high, b) + mm(a_low, b)


def by_map(a, b):
    return dot2(a, b) if b.dtype == BF16 else dot3(a, b)


def below(top, rows):
    return jnp.concatenate([jnp.zeros((top, rows.shape[1]), F32), rows.astype(F32)], axis=0)


def unit_inverse(low, rows, cols):
    size = low.shape[0]
    eye = (rows == cols).astype(F32)
    base = jnp.where(rows // 8 == cols // 8, low, 0.0)
    square = dot3(base, base)
    fourth = dot3(square, square)
    result = dot3(dot3(eye - base, eye + square), eye + fourth)
    width = 8
    while width < size:
        mask = (rows // (2 * width) == cols // (2 * width)) & (rows // width > cols // width)
        corner = jnp.where(mask, low, 0.0)
        result = result - dot3(dot3(result, corner), result)
        width *= 2
    return result


def kernel(
    nx, ny, nz,
    tok_hbm, wq_hbm, wk_hbm, wv_hbm, gate_hbm, beta_hbm, gain_hbm, wo_hbm,
    out_ref,
    tok_all, wq, wk, wv, wo_all, gate_ref, beta_ref, gain_ref, ex_send, ex_recv, gz, gy, st_send, st_recv,
    norm_all, eff, intra,
    load_sem, x_send, x_recv, wo_send, wo_recv, n_send, n_recv, core_send, core_recv,
    z_send, z_recv, y_send, y_recv,
):
    index = lax.axis_index("seq")
    x = lax.axis_index("head")
    core = index % 2
    z = (index // 2) % nz
    y = index // (2 * nz)
    size = gain_ref.shape[1]
    n_tok, width = tok_hbm.shape
    out_cols = out_ref.shape[1]

    def at(to_y, to_z, to_core, to_x):
        return ((to_y * nz + to_z) * 2 + to_core, to_x)

    x_right, x_left = at(y, z, core, (x + 1) % nx), at(y, z, core, (x + nx - 1) % nx)

    def z_to(d):
        return at(y, (z + d + nz) % nz, core, x)

    def y_to(d):
        return at((y + d + ny) % ny, z, core, x)

    partner = at(y, z, 1 - core, x)

    friends = [at(y, z, core, (x + d) % nx) for d in range(1, nx)]
    friends += [partner]
    for count, toward in ((nz, z_to), (ny, y_to)):
        steps = {d % count for d in ((1, -1, 2, -2) if count == 8 else (1, -1))} - {0}
        friends += [toward(d) for d in sorted(steps)]
    barrier = pltpu.get_barrier_semaphore()
    for friend in friends:
        pl.semaphore_signal(barrier, inc=1, device_id=friend, device_id_type=MESH)

    own_cols = pl.ds(pl.multiple_of(x * out_cols, 128), out_cols)
    loads = [
        pltpu.make_async_copy(source, target, load_sem.at[i])
        for i, (source, target) in enumerate(
            (
                (tok_hbm, tok_all.at[x]), (gate_hbm, gate_ref), (beta_hbm, beta_ref), (wk_hbm, wk),
                (wv_hbm, wv), (wq_hbm, wq), (gain_hbm, gain_ref), (wo_hbm.at[:, own_cols], wo_all.at[x]),
            )
        )
    ]
    for load in loads:
        load.start()
    pl.semaphore_wait(barrier, len(friends))

    def send(source, target, s_sem, r_sem, to):
        return pltpu.make_async_remote_copy(
            src_ref=source, dst_ref=target, send_sem=s_sem, recv_sem=r_sem,
            device_id=to, device_id_type=MESH,
        )

    def x_gather(own, slots, s_sems, r_sems, use):
        half = own.shape[0] // 2
        before, after, across = (x + nx - 1) % nx, (x + 1) % nx, (x + 2) % nx
        first, second = [], []
        for k, part in enumerate((0, half)):
            other = half - part
            first.append(
                send(own.at[pl.ds(part, half)], slots.at[x, pl.ds(part, half)], s_sems.at[0, k], r_sems.at[0, k], x_right)
            )
            second.append(
                send(own.at[pl.ds(other, half)], slots.at[x, pl.ds(other, half)], s_sems.at[1, k], r_sems.at[1, k], x_left)
            )
            first[k].start()
            second[k].start()
        use(x, None)
        first[0].wait_recv()
        top = slots.at[before, pl.ds(0, half)]
        third = send(top, top, s_sems.at[2, 0], r_sems.at[2, 0], x_right)
        third.start()
        second[0].wait_recv()
        low = slots.at[after, pl.ds(half, half)]
        fourth = send(low, low, s_sems.at[3, 0], r_sems.at[3, 0], x_left)
        fourth.start()
        first[1].wait_recv()
        use(before, slots[before])
        second[1].wait_recv()
        use(after, slots[after])
        third.wait_recv()
        fourth.wait_recv()
        use(across, slots[across])
        return first + second + [third, fourth]

    rows = lax.broadcasted_iota(jnp.int32, (n_tok, n_tok), 0)
    cols = lax.broadcasted_iota(jnp.int32, (n_tok, n_tok), 1)
    lower = rows >= cols
    r2 = lax.broadcasted_iota(jnp.int32, (2 * size, size), 0)
    c2 = lax.broadcasted_iota(jnp.int32, (2 * size, size), 1)
    unit = (r2 == c2).astype(F32)
    heads = range(2)
    logs, incls, betas, lasts = [], [], [], []

    def gates():
        loads[1].wait()
        loads[2].wait()
        ones_up = (rows <= cols).astype(BF16)
        for head in heads:
            code = -gate_ref[head : head + 1, :].astype(F32) / 2097152.0
            beta = beta_ref[head : head + 1, :].astype(F32) / 256.0
            spread = jnp.broadcast_to(code, (n_tok, n_tok))
            c_high, c_low = halves(spread)
            c_last = (spread - c_high.astype(F32) - c_low.astype(F32)).astype(BF16)
            across = mm(c_high, ones_up) + (mm(c_low, ones_up) + mm(c_last, ones_up))
            log = across.T
            gaps = log - across
            logs.append(log)
            incls.append(jnp.where(lower, jnp.exp(jnp.where(lower, gaps, 0.0)), 0.0))
            betas.append(jnp.broadcast_to(beta, (n_tok, n_tok)).T)
            lasts.append(across[0:1, n_tok - 1 : n_tok])

    sums = [jnp.zeros((n_tok, wq.shape[1]), F32) for _ in range(2)]

    def project(place, block):
        if block is None:
            gates()
            loads[0].wait()
            loads[3].wait()
            loads[4].wait()
            block = tok_all[x]
        part = pl.ds(pl.multiple_of(place * width, 128), width)
        for i, weight in enumerate((wk, wv)):
            sums[i] = sums[i] + mm(block, weight[part, :])

    tok_copies = x_gather(tok_hbm, tok_all, x_send, x_recv, project)

    out_copies = []
    for d in range(1, nx):
        there = (x + d) % nx
        there_cols = pl.ds(pl.multiple_of(there * out_cols, 128), out_cols)
        out_copies.append(
            send(wo_hbm.at[:, there_cols], wo_all.at[x], wo_send.at[d - 1], wo_recv.at[d - 1],
                 at(y, z, core, there))
        )
    for copy in out_copies:
        copy.start()

    maps, keys, solves = [], [], []
    for head in heads:
        cut = slice(head * size, (head + 1) * size)
        key, value = (s[:, cut] for s in sums)
        key = key * lax.rsqrt(jnp.sum(key * key, -1, keepdims=True) + 1e-06)
        beta, log, last = betas[head], logs[head], lasts[head]
        low = jnp.where(rows > cols, beta * dot3(key, key, ((1,), (1,))) * incls[head], 0.0)
        inverse = unit_inverse(low, rows, cols)
        right = jnp.concatenate([beta * key * jnp.exp(log), beta * value], axis=1)
        solved = dot3(inverse, right)
        tail = key * jnp.exp(last - log)
        signed = jnp.concatenate([-solved[:, :size], solved[:, size:]], axis=1)
        moved = dot3(signed, tail, ((0,), (0,)))
        maps.append(moved + jnp.where(r2 == c2, jnp.exp(last), 0.0))
        keys.append(key)
        solves.append(solved)

    first_core = core == 0
    ex_send[...] = jnp.where(first_core, maps[1], maps[0])
    swap = send(ex_send, ex_recv, core_send.at[0], core_recv.at[0], partner)
    swap.start()
    mine = jnp.where(first_core, maps[0], maps[1])
    swap.wait_recv()
    other = ex_recv[...]
    early = jnp.where(first_core, mine, other)
    late = jnp.where(first_core, other, mine)
    gz[z] = (dot3(early, late[:size]) + below(size, late[size:])).astype(WIRE)

    def ring_of_eight(slots, place, s_sems, r_sems, to, fill):
        chunks = r_sems.shape[2]
        rows_each = slots.shape[1] // chunks
        copies = {}

        def go(way, distance, chunk, hops):
            sign = 1 - 2 * way
            slot = (place - sign * (distance - hops) + 8) % 8
            piece = slots.at[slot, pl.ds(chunk * rows_each, rows_each)]
            copy = send(
                piece, piece, s_sems.at[way, distance - 1, chunk], r_sems.at[way, distance - 1, chunk], to(sign * hops)
            )
            copy.start()
            copies[way, distance, chunk] = copy

        order = list(range(chunks))
        turns = (order, order[::-1])
        for distance in (2, 1):
            for k in order:
                for way in range(2):
                    go(way, distance, turns[way][k], distance)
        fill[0]()
        for k in order:
            for way in range(2):
                chunk = turns[way][k]
                copies[way, 2, chunk].wait_recv()
                if k < chunks // 2:
                    go(way, 4, chunk, 2)
                go(way, 3, chunk, 1)
        for work in fill[1:]:
            work()
        for (way, distance, chunk), copy in copies.items():
            if distance != 2:
                copy.wait_recv()
        return list(copies.values())

    def ring(slots, place, count, s_sems, r_sems, to, fill):
        if count == 8:
            return ring_of_eight(slots, place, s_sems, r_sems, to, fill)
        chunks = r_sems.shape[2]
        rows_each = slots.shape[1] // chunks
        far = count // 2
        sent = []
        waiting = {}
        for step in range(far):
            for chunk in range(chunks):
                for way in range(2):
                    if step == far - 1 and (chunk < chunks // 2) != (way == 0):
                        continue
                    if step:
                        waiting.pop((way, step - 1, chunk)).wait_recv()
                    slot = (place + count - step) % count if way == 0 else (place + step) % count
                    piece = slots.at[slot, pl.ds(chunk * rows_each, rows_each)]
                    copy = send(
                        piece, piece, s_sems.at[way, step, chunk], r_sems.at[way, step, chunk], to(1 - 2 * way)
                    )
                    copy.start()
                    sent.append(copy)
                    waiting[way, step, chunk] = copy
            if step < len(fill):
                fill[step]()
        for work in fill[far:]:
            work()
        for copy in waiting.values():
            copy.wait_recv()
        return sent

    queries = []

    def ask():
        loads[5].wait()
        total = jnp.zeros((n_tok, wq.shape[1]), F32)
        for place in range(nx):
            total = total + mm(tok_all[place], wq[place * width : (place + 1) * width, :])
        queries.append(total)

    def inside(head):
        query = queries[0][:, head * size : (head + 1) * size]
        dots = dot3(query, keys[head], ((1,), (1,))) * incls[head]
        inner = dot3(dots, solves[head])
        intra[head] = inner[:, size:]
        eff[head] = query * jnp.exp(logs[head]) - inner[:, :size]

    def join(left, right):
        return by_map(left, right[:size]) + below(size, right[size:])

    def pairs(slots, count):
        levels = [[slots[j] for j in range(count)]]
        while len(levels[-1]) > 1:
            level = [part.astype(F32) for part in levels[-1]]
            levels.append([join(level[j], levels[-1][j + 1]) for j in range(0, len(level), 2)])
        return levels

    def pieces(levels, place):
        found = []
        for depth in reversed(range(len(levels) - 1)):
            step = 2 ** depth
            bit = (place // step) % 2 == 1
            chosen = levels[depth][0].astype(F32)
            for j in range(2, len(levels[depth]), 2):
                chosen = jnp.where(place // (2 * step) == j // 2, levels[depth][j].astype(F32), chosen)
            found.append(jnp.where(bit, chosen, unit))
        return found

    def rest():
        for head in heads:
            inside(head)

    z_copies = ring(gz, z, nz, z_send, z_recv, z_to, [ask, rest])
    levels = pairs(gz, nz)
    gy[y] = levels[-1][0].astype(WIRE)
    prefix = []

    def before_here():
        found = pieces(levels, z)
        total = found[0]
        for part in found[1:]:
            total = dot3(total, part[:size]) + below(size, part[size:])
        prefix.append(total)

    y_copies = ring(gy, y, ny, y_send, y_recv, y_to, [before_here])
    found = pieces(pairs(gy, ny), y)
    state = found[0][size:]
    for part in found[1:] + prefix:
        state = dot3(state, part[:size]) + part[size:]
    chip = state
    second = dot3(chip, early[:size]) + early[size:]
    st_send[...] = jnp.where(first_core, second, chip)
    give = send(st_send, st_recv, core_send.at[1], core_recv.at[1], partner)
    give.start()
    kept = jnp.where(first_core, chip, second)
    loads[6].wait()
    loads[7].wait()
    give.wait_recv()
    got = st_recv[...]
    states = [jnp.where(first_core, kept, got), jnp.where(first_core, got, kept)]
    gain = gain_ref[...]
    for head in heads:
        o = intra[head] + dot3(eff[head], states[head], ((1,), (1,)))
        scale = lax.rsqrt(jnp.mean(o * o, -1, keepdims=True) + 1e-06)
        norm_all[x, :, head * size : (head + 1) * size] = (o * scale * gain).astype(BF16)

    result = [jnp.zeros((n_tok, out_cols), F32)]

    def finish(place, block):
        if block is None:
            for copy in out_copies:
                copy.wait_recv()
            block = norm_all[x]
        result[0] = result[0] + mm(block, wo_all[place])

    n_copies = x_gather(norm_all.at[x], norm_all, n_send, n_recv, finish)
    out_ref[...] = result[0].astype(BF16)
    for copy in tok_copies + out_copies + z_copies + y_copies + [swap, give] + n_copies:
        copy.wait_send()


def shards(ny, nz, nx, tokens, w_query, w_key, w_value, gate_codes, beta_codes, norm_gain, w_out):
    n_tok, width = tokens.shape
    size = norm_gain.shape[0]
    here = w_query.shape[1]
    hbm = pl.BlockSpec(memory_space=pltpu.HBM)
    chunks = 2
    dma = pltpu.SemaphoreType.DMA
    return pl.pallas_call(
        functools.partial(kernel, nx, ny, nz),
        out_shape=jax.ShapeDtypeStruct((n_tok, w_out.shape[1] // nx), BF16),
        in_specs=[hbm] * 8,
        out_specs=pl.BlockSpec(memory_space=pltpu.VMEM),
        scratch_shapes=[
            pltpu.VMEM((nx, n_tok, width), BF16),
            pltpu.VMEM(w_query.shape, BF16),
            pltpu.VMEM(w_key.shape, BF16),
            pltpu.VMEM(w_value.shape, BF16),
            pltpu.VMEM((nx, here, w_out.shape[1] // nx), BF16),
            pltpu.VMEM((2, n_tok), jnp.int32),
            pltpu.VMEM((2, n_tok), jnp.int32),
            pltpu.VMEM((1, size), F32),
            pltpu.VMEM((2 * size, size), F32),
            pltpu.VMEM((2 * size, size), F32),
            pltpu.VMEM((nz, 2 * size, size), WIRE),
            pltpu.VMEM((ny, 2 * size, size), WIRE),
            pltpu.VMEM((size, size), F32),
            pltpu.VMEM((size, size), F32),
            pltpu.VMEM((nx, n_tok, here), BF16),
            pltpu.VMEM((2, n_tok, size), F32),
            pltpu.VMEM((2, n_tok, size), F32),
            dma((8,)), dma((4, 2)), dma((4, 2)), dma((nx - 1,)), dma((nx - 1,)), dma((4, 2)), dma((4, 2)),
            dma((2,)), dma((2,)), dma((2, nz, chunks)), dma((2, nz, chunks)), dma((2, ny, chunks)),
            dma((2, ny, chunks)),
        ],
        compiler_params=pltpu.CompilerParams(
            collective_id=0, has_side_effects=True, vmem_limit_bytes=67043328
        ),
    )(tokens, w_query, w_key, w_value, gate_codes.T, beta_codes.T, norm_gain.reshape(1, size), w_out)


def along_z(chips):
    nz = 1
    while nz * nz < chips:
        nz *= 2
    return nz


def solution(mesh):
    chips = mesh.shape["seq"] // 2
    nz = along_z(chips)
    return jax.shard_map(
        functools.partial(shards, chips // nz, nz, mesh.shape["head"]),
        mesh=mesh,
        in_specs=(
            P("seq", "head"), P(None, "head"), P(None, "head"), P(None, "head"),
            P("seq", "head"), P("seq", "head"), P(), P("head", None),
        ),
        out_specs=P("seq", "head"),
        check_vma=False,
    )
```

```python
import functools
import jax
import jax.numpy as jnp
from jax import lax
from jax.experimental import pallas as pl
from jax.experimental.pallas import tpu as pltpu
from jax.sharding import PartitionSpec as P

MESH = pl.DeviceIdType.MESH
WIRE = jnp.bfloat16
F32 = jnp.float32
BF16 = jnp.bfloat16


def mm(a, b, dims=((1,), (0,))):
    return lax.dot_general(a, b, (dims, ((), ())), preferred_element_type=F32)


def halves(a):
    high = a.astype(BF16)
    return high, (a - high.astype(F32)).astype(BF16)


def dot3(a, b, dims=((1,), (0,))):
    a_high, a_low = halves(a)
    b_high, b_low = halves(b)
    free = 1 - dims[1][0]
    count = b.shape[free]
    both = mm(a_high, jnp.concatenate([b_high, b_low], axis=free), dims)
    return both[:, :count] + (both[:, count:] + mm(a_low, b_high, dims))


def dot2(a, b):
    a_high, a_low = halves(a)
    return mm(a_high, b) + mm(a_low, b)


def by_map(a, b):
    return dot2(a, b) if b.dtype == BF16 else dot3(a, b)


def below(top, rows):
    return jnp.concatenate([jnp.zeros((top, rows.shape[1]), F32), rows.astype(F32)], axis=0)


def unit_inverse(low, rows, cols):
    size = low.shape[0]
    eye = (rows == cols).astype(F32)
    base = jnp.where(rows // 8 == cols // 8, low, 0.0)
    square = dot3(base, base)
    fourth = dot3(square, square)
    result = dot3(dot3(eye - base, eye + square), eye + fourth)
    width = 8
    while width < size:
        mask = (rows // (2 * width) == cols // (2 * width)) & (rows // width > cols // width)
        corner = jnp.where(mask, low, 0.0)
        result = result - dot3(dot3(result, corner), result)
        width *= 2
    return result


def kernel(
    nx, ny, nz,
    tok_hbm, wq_hbm, wk_hbm, wv_hbm, gate_hbm, beta_hbm, gain_hbm, wo_hbm,
    out_ref,
    tok_all, wq, wk, wv, wo_all, gate_ref, beta_ref, gain_ref, ex_send, ex_recv, gz, gy, st_send, st_recv,
    norm_all, eff, intra,
    load_sem, x_send, x_recv, wo_send, wo_recv, n_send, n_recv, core_send, core_recv,
    z_send, z_recv, y_send, y_recv,
):
    index = lax.axis_index("seq")
    x = lax.axis_index("head")
    core = index % 2
    z = (index // 2) % nz
    y = index // (2 * nz)
    size = gain_ref.shape[1]
    n_tok, width = tok_hbm.shape
    out_cols = out_ref.shape[1]

    def at(to_y, to_z, to_core, to_x):
        return ((to_y * nz + to_z) * 2 + to_core, to_x)

    x_right, x_left = at(y, z, core, (x + 1) % nx), at(y, z, core, (x + nx - 1) % nx)

    def z_to(d):
        return at(y, (z + d + nz) % nz, core, x)

    def y_to(d):
        return at((y + d + ny) % ny, z, core, x)

    partner = at(y, z, 1 - core, x)

    friends = [at(y, z, core, (x + d) % nx) for d in range(1, nx)]
    friends += [partner]
    for count, toward in ((nz, z_to), (ny, y_to)):
        steps = {d % count for d in ((1, -1, 2, -2) if count == 8 else (1, -1))} - {0}
        friends += [toward(d) for d in sorted(steps)]
    barrier = pltpu.get_barrier_semaphore()
    for friend in friends:
        pl.semaphore_signal(barrier, inc=1, device_id=friend, device_id_type=MESH)

    own_cols = pl.ds(pl.multiple_of(x * out_cols, 128), out_cols)
    loads = [
        pltpu.make_async_copy(source, target, load_sem.at[i])
        for i, (source, target) in enumerate(
            (
                (tok_hbm, tok_all.at[x]), (gate_hbm, gate_ref), (beta_hbm, beta_ref), (wk_hbm, wk),
                (wv_hbm, wv), (wq_hbm, wq), (gain_hbm, gain_ref), (wo_hbm.at[:, own_cols], wo_all.at[x]),
            )
        )
    ]
    for load in loads:
        load.start()
    pl.semaphore_wait(barrier, len(friends))

    def send(source, target, s_sem, r_sem, to):
        return pltpu.make_async_remote_copy(
            src_ref=source, dst_ref=target, send_sem=s_sem, recv_sem=r_sem,
            device_id=to, device_id_type=MESH,
        )

    def x_gather(own, slots, s_sems, r_sems, use):
        half = own.shape[0] // 2
        before, after, across = (x + nx - 1) % nx, (x + 1) % nx, (x + 2) % nx
        first, second = [], []
        for k, part in enumerate((0, half)):
            other = half - part
            first.append(
                send(own.at[pl.ds(part, half)], slots.at[x, pl.ds(part, half)], s_sems.at[0, k], r_sems.at[0, k], x_right)
            )
            second.append(
                send(own.at[pl.ds(other, half)], slots.at[x, pl.ds(other, half)], s_sems.at[1, k], r_sems.at[1, k], x_left)
            )
            first[k].start()
            second[k].start()
        use(x, None)
        first[0].wait_recv()
        top = slots.at[before, pl.ds(0, half)]
        third = send(top, top, s_sems.at[2, 0], r_sems.at[2, 0], x_right)
        third.start()
        second[0].wait_recv()
        low = slots.at[after, pl.ds(half, half)]
        fourth = send(low, low, s_sems.at[3, 0], r_sems.at[3, 0], x_left)
        fourth.start()
        first[1].wait_recv()
        use(before, slots[before])
        second[1].wait_recv()
        use(after, slots[after])
        third.wait_recv()
        fourth.wait_recv()
        use(across, slots[across])
        return first + second + [third, fourth]

    rows = lax.broadcasted_iota(jnp.int32, (n_tok, n_tok), 0)
    cols = lax.broadcasted_iota(jnp.int32, (n_tok, n_tok), 1)
    lower = rows >= cols
    r2 = lax.broadcasted_iota(jnp.int32, (2 * size, size), 0)
    c2 = lax.broadcasted_iota(jnp.int32, (2 * size, size), 1)
    unit = (r2 == c2).astype(F32)
    heads = range(2)
    logs, incls, betas, lasts = [], [], [], []

    def gates():
        loads[1].wait()
        loads[2].wait()
        ones_up = (rows <= cols).astype(BF16)
        for head in heads:
            code = -gate_ref[head : head + 1, :].astype(F32) / 2097152.0
            beta = beta_ref[head : head + 1, :].astype(F32) / 256.0
            spread = jnp.broadcast_to(code, (n_tok, n_tok))
            c_high, c_low = halves(spread)
            c_last = (spread - c_high.astype(F32) - c_low.astype(F32)).astype(BF16)
            across = mm(c_high, ones_up) + (mm(c_low, ones_up) + mm(c_last, ones_up))
            log = across.T
            gaps = log - across
            logs.append(log)
            incls.append(jnp.where(lower, jnp.exp(jnp.where(lower, gaps, 0.0)), 0.0))
            betas.append(jnp.broadcast_to(beta, (n_tok, n_tok)).T)
            lasts.append(across[0:1, n_tok - 1 : n_tok])

    sums = [jnp.zeros((n_tok, wq.shape[1]), F32) for _ in range(2)]

    def project(place, block):
        if block is None:
            gates()
            loads[0].wait()
            loads[3].wait()
            loads[4].wait()
            block = tok_all[x]
        part = pl.ds(pl.multiple_of(place * width, 128), width)
        for i, weight in enumerate((wk, wv)):
            sums[i] = sums[i] + mm(block, weight[part, :])

    tok_copies = x_gather(tok_hbm, tok_all, x_send, x_recv, project)

    out_copies = []
    for d in range(1, nx):
        there = (x + d) % nx
        there_cols = pl.ds(pl.multiple_of(there * out_cols, 128), out_cols)
        out_copies.append(
            send(wo_hbm.at[:, there_cols], wo_all.at[x], wo_send.at[d - 1], wo_recv.at[d - 1],
                 at(y, z, core, there))
        )

    maps, keys, solves = [], [], []
    for head in heads:
        cut = slice(head * size, (head + 1) * size)
        key, value = (s[:, cut] for s in sums)
        key = key * lax.rsqrt(jnp.sum(key * key, -1, keepdims=True) + 1e-06)
        beta, log, last = betas[head], logs[head], lasts[head]
        low = jnp.where(rows > cols, beta * dot3(key, key, ((1,), (1,))) * incls[head], 0.0)
        inverse = unit_inverse(low, rows, cols)
        right = jnp.concatenate([beta * key * jnp.exp(log), beta * value], axis=1)
        solved = dot3(inverse, right)
        tail = key * jnp.exp(last - log)
        signed = jnp.concatenate([-solved[:, :size], solved[:, size:]], axis=1)
        moved = dot3(signed, tail, ((0,), (0,)))
        maps.append(moved + jnp.where(r2 == c2, jnp.exp(last), 0.0))
        keys.append(key)
        solves.append(solved)

    first_core = core == 0
    ex_send[...] = jnp.where(first_core, maps[1], maps[0])
    swap = send(ex_send, ex_recv, core_send.at[0], core_recv.at[0], partner)
    swap.start()
    for copy in out_copies:
        copy.start()
    mine = jnp.where(first_core, maps[0], maps[1])
    swap.wait_recv()
    other = ex_recv[...]
    early = jnp.where(first_core, mine, other)
    late = jnp.where(first_core, other, mine)
    gz[z] = (dot3(early, late[:size]) + below(size, late[size:])).astype(WIRE)

    def ring_of_eight(slots, place, s_sems, r_sems, to, fill):
        chunks = r_sems.shape[2]
        rows_each = slots.shape[1] // chunks
        copies = {}

        def go(way, distance, chunk, hops):
            sign = 1 - 2 * way
            slot = (place - sign * (distance - hops) + 8) % 8
            piece = slots.at[slot, pl.ds(chunk * rows_each, rows_each)]
            copy = send(
                piece, piece, s_sems.at[way, distance - 1, chunk], r_sems.at[way, distance - 1, chunk], to(sign * hops)
            )
            copy.start()
            copies[way, distance, chunk] = copy

        order = list(range(chunks))
        turns = (order, order[::-1])
        for distance in (2, 1):
            for k in order:
                for way in range(2):
                    go(way, distance, turns[way][k], distance)
        fill[0]()
        for k in order:
            for way in range(2):
                chunk = turns[way][k]
                copies[way, 2, chunk].wait_recv()
                if k < chunks // 2:
                    go(way, 4, chunk, 2)
                go(way, 3, chunk, 1)
        for work in fill[1:]:
            work()
        for (way, distance, chunk), copy in copies.items():
            if distance != 2:
                copy.wait_recv()
        return list(copies.values())

    def ring(slots, place, count, s_sems, r_sems, to, fill):
        if count == 8:
            return ring_of_eight(slots, place, s_sems, r_sems, to, fill)
        chunks = r_sems.shape[2]
        rows_each = slots.shape[1] // chunks
        far = count // 2
        sent = []
        waiting = {}
        for step in range(far):
            for chunk in range(chunks):
                for way in range(2):
                    if step == far - 1 and (chunk < chunks // 2) != (way == 0):
                        continue
                    if step:
                        waiting.pop((way, step - 1, chunk)).wait_recv()
                    slot = (place + count - step) % count if way == 0 else (place + step) % count
                    piece = slots.at[slot, pl.ds(chunk * rows_each, rows_each)]
                    copy = send(
                        piece, piece, s_sems.at[way, step, chunk], r_sems.at[way, step, chunk], to(1 - 2 * way)
                    )
                    copy.start()
                    sent.append(copy)
                    waiting[way, step, chunk] = copy
            if step < len(fill):
                fill[step]()
        for work in fill[far:]:
            work()
        for copy in waiting.values():
            copy.wait_recv()
        return sent

    queries = []

    def ask():
        loads[5].wait()
        total = jnp.zeros((n_tok, wq.shape[1]), F32)
        for place in range(nx):
            total = total + mm(tok_all[place], wq[place * width : (place + 1) * width, :])
        queries.append(total)

    def inside(head):
        query = queries[0][:, head * size : (head + 1) * size]
        dots = dot3(query, keys[head], ((1,), (1,))) * incls[head]
        inner = dot3(dots, solves[head])
        intra[head] = inner[:, size:]
        eff[head] = query * jnp.exp(logs[head]) - inner[:, :size]

    def join(left, right):
        return by_map(left, right[:size]) + below(size, right[size:])

    def pairs(slots, count):
        levels = [[slots[j] for j in range(count)]]
        while len(levels[-1]) > 1:
            level = [part.astype(F32) for part in levels[-1]]
            levels.append([join(level[j], levels[-1][j + 1]) for j in range(0, len(level), 2)])
        return levels

    def pieces(levels, place):
        found = []
        for depth in reversed(range(len(levels) - 1)):
            step = 2 ** depth
            bit = (place // step) % 2 == 1
            chosen = levels[depth][0].astype(F32)
            for j in range(2, len(levels[depth]), 2):
                chosen = jnp.where(place // (2 * step) == j // 2, levels[depth][j].astype(F32), chosen)
            found.append(jnp.where(bit, chosen, unit))
        return found

    def rest():
        for head in heads:
            inside(head)

    z_copies = ring(gz, z, nz, z_send, z_recv, z_to, [ask, rest])
    levels = pairs(gz, nz)
    gy[y] = levels[-1][0].astype(WIRE)
    prefix = []

    def before_here():
        found = pieces(levels, z)
        total = found[0]
        for part in found[1:]:
            total = dot3(total, part[:size]) + below(size, part[size:])
        prefix.append(total)

    y_copies = ring(gy, y, ny, y_send, y_recv, y_to, [before_here])
    found = pieces(pairs(gy, ny), y)
    state = found[0][size:]
    for part in found[1:] + prefix:
        state = dot3(state, part[:size]) + part[size:]
    chip = state
    second = dot3(chip, early[:size]) + early[size:]
    st_send[...] = jnp.where(first_core, second, chip)
    give = send(st_send, st_recv, core_send.at[1], core_recv.at[1], partner)
    give.start()
    kept = jnp.where(first_core, chip, second)
    loads[6].wait()
    loads[7].wait()
    give.wait_recv()
    got = st_recv[...]
    states = [jnp.where(first_core, kept, got), jnp.where(first_core, got, kept)]
    gain = gain_ref[...]
    for head in heads:
        o = intra[head] + dot3(eff[head], states[head], ((1,), (1,)))
        scale = lax.rsqrt(jnp.mean(o * o, -1, keepdims=True) + 1e-06)
        norm_all[x, :, head * size : (head + 1) * size] = (o * scale * gain).astype(BF16)

    result = [jnp.zeros((n_tok, out_cols), F32)]

    def finish(place, block):
        if block is None:
            for copy in out_copies:
                copy.wait_recv()
            block = norm_all[x]
        result[0] = result[0] + mm(block, wo_all[place])

    n_copies = x_gather(norm_all.at[x], norm_all, n_send, n_recv, finish)
    out_ref[...] = result[0].astype(BF16)
    for copy in tok_copies + out_copies + z_copies + y_copies + [swap, give] + n_copies:
        copy.wait_send()


def shards(ny, nz, nx, tokens, w_query, w_key, w_value, gate_codes, beta_codes, norm_gain, w_out):
    n_tok, width = tokens.shape
    size = norm_gain.shape[0]
    here = w_query.shape[1]
    hbm = pl.BlockSpec(memory_space=pltpu.HBM)
    chunks = 2
    dma = pltpu.SemaphoreType.DMA
    return pl.pallas_call(
        functools.partial(kernel, nx, ny, nz),
        out_shape=jax.ShapeDtypeStruct((n_tok, w_out.shape[1] // nx), BF16),
        in_specs=[hbm] * 8,
        out_specs=pl.BlockSpec(memory_space=pltpu.VMEM),
        scratch_shapes=[
            pltpu.VMEM((nx, n_tok, width), BF16),
            pltpu.VMEM(w_query.shape, BF16),
            pltpu.VMEM(w_key.shape, BF16),
            pltpu.VMEM(w_value.shape, BF16),
            pltpu.VMEM((nx, here, w_out.shape[1] // nx), BF16),
            pltpu.VMEM((2, n_tok), jnp.int32),
            pltpu.VMEM((2, n_tok), jnp.int32),
            pltpu.VMEM((1, size), F32),
            pltpu.VMEM((2 * size, size), F32),
            pltpu.VMEM((2 * size, size), F32),
            pltpu.VMEM((nz, 2 * size, size), WIRE),
            pltpu.VMEM((ny, 2 * size, size), WIRE),
            pltpu.VMEM((size, size), F32),
            pltpu.VMEM((size, size), F32),
            pltpu.VMEM((nx, n_tok, here), BF16),
            pltpu.VMEM((2, n_tok, size), F32),
            pltpu.VMEM((2, n_tok, size), F32),
            dma((8,)), dma((4, 2)), dma((4, 2)), dma((nx - 1,)), dma((nx - 1,)), dma((4, 2)), dma((4, 2)),
            dma((2,)), dma((2,)), dma((2, nz, chunks)), dma((2, nz, chunks)), dma((2, ny, chunks)),
            dma((2, ny, chunks)),
        ],
        compiler_params=pltpu.CompilerParams(
            collective_id=0, has_side_effects=True, vmem_limit_bytes=67043328
        ),
    )(tokens, w_query, w_key, w_value, gate_codes.T, beta_codes.T, norm_gain.reshape(1, size), w_out)


def along_z(chips):
    nz = 1
    while nz * nz < chips:
        nz *= 2
    return nz


def solution(mesh):
    chips = mesh.shape["seq"] // 2
    nz = along_z(chips)
    return jax.shard_map(
        functools.partial(shards, chips // nz, nz, mesh.shape["head"]),
        mesh=mesh,
        in_specs=(
            P("seq", "head"), P(None, "head"), P(None, "head"), P(None, "head"),
            P("seq", "head"), P("seq", "head"), P(), P("head", None),
        ),
        out_specs=P("seq", "head"),
        check_vma=False,
    )
```
